256 devices in a mesh: page: 32 (over x, z), tok: 8 (over y, core).
Axes of the slice: x: 4, y: 4, z: 8, core: 2. Of those that a mesh axis runs over, the one named last changes fastest.
Arguments:
- tile_tokens: bfloat16 [32, 4096, 1024], P('page', 'tok'), may hold values from -6 to 6
- page_lengths: int32 [32], P('page'), may hold values from 1 to 4096, as said below
- occupancy: int32 [32, 32], P('page', 'tok'), may hold values 0 or 1
- block_mix: bfloat16 [32, 128, 128], P('tok'), may hold values from -0.5 to 0.5
- stride_mix: bfloat16 [128, 32, 32], P('tok'), may hold values from -1 to 1
- w_gate_up: bfloat16 [2, 1024, 2048], P(None, None, ('page', 'tok')), may hold values from -0.1875 to 0.1875
- w_down: bfloat16 [2048, 1024], P(None, ('page', 'tok')), may hold values from -0.125 to 0.125
Outputs:
- packed_lanes: bfloat16 [8, 16384, 1024], P('tok', 'page')
The draws below stay inside these ranges and needn't reach their ends.
Inputs may be any that keep to these rules, and one draw needn't show every extreme that they name: `page_lengths`: some page has exactly 4096 used tokens in every draw; page 0 has fewer than 512 used tokens in every draw.
All inputs are finite; a program needn't handle non-finite values. No bound on the sum of `occupancy` on one device may be relied on, other than what follows from the above.
Results may differ from the reference program's by a relative error of at most 0.012.
Values may be sent and summed in bfloat16 or wider, within the bound.
A program may use at most 64 MiB of HBM per device.

```python
import jax
import jax.numpy as jnp
from jax import lax

D = 1024
FF = 2048
BLK = 128
NB = 32
PAGE_LEN = 4096
N_PAGE = 32
N_TOK = 8


def draw_page_lengths(key, part):
    full_len = NB * BLK
    lane_rows = full_len // N_TOK
    key_one, key_two, key_top, key_head = jax.random.split(key, 4)
    draw_one = jax.random.randint(key_one, (N_PAGE,), 1, full_len + 1)
    draw_two = jax.random.randint(key_two, (N_PAGE,), 1, full_len + 1)
    lengths = jnp.minimum(draw_one, draw_two)
    head_len = jax.random.randint(key_head, (), 1, lane_rows)
    longest = jax.random.randint(key_top, (), 1, N_PAGE)
    page_ids = jnp.arange(N_PAGE)
    lengths = jnp.where(page_ids == 0, head_len, lengths)
    return jnp.where(page_ids == longest, full_len, lengths).astype(jnp.int32)


def touch_ends(values, key, least, high):
    place = [jax.random.randint(jax.random.fold_in(key, axis), (), 0, length) for axis, length in enumerate(values.shape)]
    widest = values.shape.index(max(values.shape))
    neighbour = place[:widest] + [(place[widest] + 1) % values.shape[widest]] + place[widest + 1:]
    return values.at[tuple(place)].set(least).at[tuple(neighbour)].set(high)


def steps_of(own_key, extent, shards, least, high):
    def one(dim, parts):
        draws = jax.random.uniform(jax.random.fold_in(jax.random.fold_in(own_key, 6), dim), (parts,), jnp.float32, least / len(shards), high / len(shards))
        return jnp.repeat(jnp.exp(draws), extent[dim] // parts).reshape((-1,) + (1,) * (len(extent) - dim - 1))

    loudness = one(*shards[0])
    for cut in shards[1:]:
        loudness = loudness * one(*cut)
    return loudness


def scatter_about(rng, extent, scale, reach, cuts=(), kind=jnp.bfloat16):
    gain = steps_of(rng, extent, cuts, -0.22, 0.18) if cuts else 1.0
    drawn = jax.random.normal(rng, extent, jnp.float32) * scale * gain
    return jnp.minimum(jnp.maximum(drawn, -reach), reach).astype(kind)


def setup_inputs(seed: int = 0) -> dict:
    arg_keys = jax.random.split(jax.random.key(seed), 8)
    return {
        "tile_tokens": scatter_about(arg_keys[0], (N_PAGE, PAGE_LEN, D), 1.0, 6.0, ((0, 32), (1, 8))),
        "page_lengths": draw_page_lengths(jax.random.fold_in(arg_keys[7], 71), 0),
        "occupancy": touch_ends((jax.random.randint(arg_keys[2], (N_PAGE, NB), 0, 4) < 3).astype(jnp.int32), jax.random.fold_in(arg_keys[2], 1), 0, 1),
        "block_mix": scatter_about(arg_keys[3], (NB, BLK, BLK), BLK ** -0.5, 0.5, ((0, 8),)),
        "stride_mix": scatter_about(arg_keys[4], (BLK, NB, NB), NB ** -0.5, 1.0, ((0, 8),)),
        "w_gate_up": scatter_about(arg_keys[5], (2, D, FF), D ** -0.5, 0.1875, ((2, 256),)),
        "w_down": scatter_about(arg_keys[6], (FF, D), FF ** -0.5, 0.125, ((1, 256),)),
    }


epsilon = 1e-05

def rms_round(values):
    scale = lax.rsqrt(lax.optimization_barrier(jnp.mean(values * values, axis=-1, keepdims=True)) + epsilon)
    return (values * scale).astype(jnp.bfloat16)

def one_page(inputs, block_mix, stride_mix, w_gate_up, w_down):
    tile_rows, length, occ_row = inputs
    page_len = NB * BLK
    positions = jnp.arange(page_len, dtype=jnp.int32)
    live_mask = (positions < length) & (jnp.repeat(occ_row, BLK) > 0)
    masked = jnp.where(live_mask[:, None], tile_rows.astype(jnp.float32), 0.0)
    normed = rms_round(masked).reshape(NB, BLK, D)
    first = jnp.einsum('bji,bic->bjc', block_mix.astype(jnp.float32), normed.astype(jnp.float32)).astype(jnp.bfloat16)
    second = jnp.einsum('jkb,bjc->jkc', stride_mix.astype(jnp.float32), first.astype(jnp.float32))
    mixed = (masked + second.reshape(page_len, D)).astype(jnp.bfloat16)
    mixed_float = mixed.astype(jnp.float32)
    normed_two = rms_round(mixed_float)
    gate_vals = jnp.dot(normed_two, w_gate_up[0], preferred_element_type=jnp.float32)
    up_vals = jnp.dot(normed_two, w_gate_up[1], preferred_element_type=jnp.float32)
    hidden = (jax.nn.silu(gate_vals) * up_vals).astype(jnp.bfloat16)
    down_vals = jnp.dot(hidden, w_down, preferred_element_type=jnp.float32)
    return (mixed_float + down_vals).astype(jnp.bfloat16)

def reference(tile_tokens, page_lengths, occupancy, block_mix, stride_mix, w_gate_up, w_down):
    layer_out = lax.map(lambda inputs: one_page(inputs, block_mix, stride_mix, w_gate_up, w_down), (tile_tokens, page_lengths, occupancy))
    lane_count = N_TOK
    row_count = NB * BLK // lane_count
    lane_index = jnp.arange(lane_count, dtype=jnp.int32)
    kept = jnp.clip(page_lengths[:, None] - lane_index[None, :] * row_count, 0, row_count).astype(jnp.int32)
    offset = (jnp.cumsum(kept, axis=0) - kept).astype(jnp.int32)
    rows_in = jnp.arange(row_count, dtype=jnp.int32)
    total_rows = N_PAGE * row_count
    target = offset[:, :, None] + rows_in[None, None, :]
    target = jnp.where(rows_in[None, None, :] < kept[:, :, None], target, total_rows).astype(jnp.int32)
    pieces = layer_out.reshape(N_PAGE, lane_count, row_count, D)

    def one_lane(lane):
        dest = lax.dynamic_index_in_dim(target, lane, 1, keepdims=False).reshape(-1)
        rows_here = lax.dynamic_index_in_dim(pieces, lane, 1, keepdims=False).reshape(-1, D)
        empty = jnp.zeros((total_rows, D), jnp.bfloat16)
        return empty.at[dest].set(rows_here, mode='drop')
    return lax.map(one_lane, lane_index)
```

```python
import jax
import jax.numpy as jnp
from jax import lax
from jax.experimental import pallas as pl
from jax.experimental.pallas import tpu as pltpu
from jax.sharding import PartitionSpec as P

NX, NZ, NY, NC = 4, 8, 4, 2
PAGES, TOKS = 32, 8
ROWS, D, FF = 512, 1024, 2048
BLK, NB, PER = 128, 32, 16
EPS = 1e-05
MESH = pl.DeviceIdType.MESH
NT = (((1,), (1,)), ((), ()))
BF, F32 = jnp.bfloat16, jnp.float32


def mod(a, n):
    return lax.rem(a, jnp.int32(n))


def div(a, n):
    return lax.div(a, jnp.int32(n))


def iota(shape, dim):
    return lax.broadcasted_iota(jnp.int32, shape, dim)


def matmul(a, b):
    return jnp.dot(a, b, preferred_element_type=F32)


def matmul_nt(a, b):
    return lax.dot_general(a, b, NT, preferred_element_type=F32)


def rms_round(values):
    scale = lax.rsqrt(jnp.mean(values * values, axis=-1, keepdims=True) + EPS)
    return (values * scale).astype(BF)


def body(
    len_ref, occ_ref, x_ref, bm_ref, sm_ref, wg_ref, wd_ref, o_ref,
    lens_rx, gu_tx, gu_rx, wd_tx, wd_rx, w, fsend, frecv, xm, spread, pre, psel,
    p1tx, p1rx, ymix, ynorm, hid, p2tx,
    lens_s, lens_r, gu_s, gu_r, wd_s, wd_r, z_s, z_r, tok_s, tok_r,
    p1_s, p1_r, p2_s, p2_r, ring_s, ring_r, core_s, core_r, own_s,
):
    page, tok = lax.axis_index("page"), lax.axis_index("tok")
    x, z = div(page, NZ), mod(page, NZ)
    y, c = div(tok, NC), mod(tok, NC)
    yh, yl = div(y, 2), mod(y, 2)
    sibling = tok + 1 - 2 * c

    def rcopy(src, dst, ssem, rsem, to_page, to_tok):
        return pltpu.make_async_remote_copy(
            src_ref=src, dst_ref=dst, send_sem=ssem, recv_sem=rsem,
            device_id=(to_page, to_tok), device_id_type=MESH,
        )

    def wait_recv(ref, sem):
        rcopy(ref, ref, sem, sem, page, sibling).wait_recv()

    def wait_send(ref, sem):
        rcopy(ref, ref, sem, sem, page, sibling).wait_send()

    barrier = pltpu.get_barrier_semaphore()

    @pl.loop(1, PAGES)
    def _(k):
        pl.semaphore_signal(barrier, inc=1, device_id=(mod(page + k, PAGES), tok), device_id_type=MESH)

    @pl.loop(1, TOKS)
    def _(k):
        pl.semaphore_signal(barrier, inc=1, device_id=(page, mod(tok + k, TOKS)), device_id_type=MESH)

    length = len_ref[0]
    place8 = (iota((16, 8), 0) == iota((16, 8), 1) + 8 * c).astype(BF)
    place4 = (iota((16, 4), 0) == iota((16, 4), 1) + 4 * mod(tok, 4)).astype(BF)
    for g in range(2):
        gu_tx[g] = matmul(place8, wg_ref[g]).astype(BF)
    wd_all = matmul(place4, wd_ref[...]).astype(BF)
    for q in range(4):
        wd_tx[q] = wd_all[:, q * 512 : (q + 1) * 512]
    lens_rx[page] = jnp.full((8, 128), length, jnp.int32)

    pl.semaphore_wait(barrier, PAGES - 1 + TOKS - 1)

    rcopy(gu_tx.at[1 - c], gu_rx, gu_s, gu_r, page, sibling).start()
    half = 4 * div(tok, 4)
    for k in range(1, 4):
        q = mod(tok + k, 4)
        rcopy(wd_tx.at[q], wd_rx.at[3 - k], wd_s, wd_r, page, half + q).start()

    @pl.loop(1, PAGES)
    def _(k):
        rcopy(lens_rx.at[page], lens_rx.at[page], lens_s, lens_r, mod(page + k, PAGES), tok).start()

    for b in range(4):
        limit = length * occ_ref[0, b] - tok * ROWS - b * BLK
        rows = slice(b * BLK, (b + 1) * BLK)
        live = iota((BLK, D), 0) < limit
        masked = jnp.where(live, x_ref[rows, :].astype(F32), 0.0)
        xm[rows, :] = masked.astype(BF)
        first = matmul(bm_ref[b], rms_round(masked)).astype(BF)
        fsend[:, b] = first.reshape(TOKS, PER, D)

    @pl.loop(1, TOKS)
    def _(k):
        to = mod(tok + k, TOKS)
        rcopy(fsend.at[to], frecv.at[tok], tok_s, tok_r, page, to).start()

    own_first = pltpu.make_async_copy(fsend.at[tok], frecv.at[tok], own_s.at[0])
    own_first.start()

    wait_recv(gu_rx, gu_r)
    wait_recv(wd_rx, wd_r)
    w[c, x, z, yh, yl, :, 0:D] = gu_tx[c] + gu_rx[...]
    w[c, x, z, yh, yl, :, D:] = wd_tx[mod(tok, 4)] + wd_rx[0] + wd_rx[1] + wd_rx[2]

    @pl.loop(1, NZ)
    def _(k):
        unit = w.at[c, x, z, yh, yl]
        rcopy(unit, unit, z_s, z_r, x * NZ + mod(z + k, NZ), tok).start()

    expand = (iota((NB, ROWS), 0) == iota((NB, ROWS), 1) // PER).astype(BF)
    wide = matmul(sm_ref[...].reshape(ROWS, NB), expand)
    same = iota((ROWS, ROWS), 1) % PER == iota((ROWS, ROWS), 0) // 32
    spread[...] = jnp.where(same, wide, 0.0).astype(BF)

    wait_recv(lens_rx.at[pl.ds(0, PAGES - 1)], lens_r)
    lens = lens_rx[:, 0, :]
    lens = jnp.concatenate([lens] * 4, axis=1)
    kept = jnp.clip(lens - tok * ROWS, 0, ROWS)
    who = iota((PAGES, ROWS), 0)
    lane_page = iota((PAGES, ROWS), 1) // PER
    shift = jnp.sum(jnp.where(who < page, kept, 0), axis=0, keepdims=True)
    start_of = jnp.sum(jnp.where(who < lane_page, kept, 0), axis=0, keepdims=True)
    stop_of = start_of + jnp.sum(jnp.where(who == lane_page, kept, 0), axis=0, keepdims=True)

    @pl.loop(0, 4)
    def _(r):
        rows = pl.ds(pl.multiple_of(r * 128, 128), 128)
        slot = iota((128, ROWS), 0) + r * 128
        turn = (((iota((128, ROWS), 1) + shift) & (ROWS - 1)) == slot).astype(BF)
        pre[rows, :] = matmul(turn, xm[...]).astype(BF)
        psel[rows, :] = matmul(turn, spread[...]).astype(BF)

    def ylo(yy, z0, n):
        return w.at[c, :, pl.ds(z0, n), div(yy, 2), mod(yy, 2)]

    def xhi(xx, z0, n):
        return w.at[c, xx, pl.ds(z0, n)]

    def xlo(xx, z0, n):
        return w.at[c, xx, pl.ds(z0, n), yh, yl]

    def yhi(yy, z0, n):
        return w.at[c, x, pl.ds(z0, n), div(yy, 2), mod(yy, 2)]

    def xdev(by):
        return mod(x + by, NX) * NZ + z, tok

    def ydev(by):
        return page, mod(y + by, NY) * NC + c

    rings = [
        [(xlo, x, xdev, 0, NX), (yhi, y, ydev, 4, NY)],
        [(ylo, y, ydev, 0, NY), (xhi, x, xdev, 4, NX)],
    ]

    def ring_copy(stage, which, hop, way):
        piece, me, dev, z0, n = rings[stage][which]
        by = 1 if way == 0 else n - 1
        if hop == 0:
            ref = piece(me, z0, 4)
        else:
            ref = piece(mod(me + n - by, n), z0 + 2 * way, 2)
        i = stage * 8 + hop * 4 + which * 2 + way
        return rcopy(ref, ref, ring_s.at[i], ring_r.at[i], *dev(by))

    def ring_arrived(stage, which, hop, way):
        piece, me, dev, z0, n = rings[stage][which]
        by = 1 if way == 0 else n - 1
        ref = piece(mod(me + n - by, n), z0, 4) if hop == 0 else piece(mod(me + 2, n), z0 + 2 * way, 2)
        wait_recv(ref, ring_r.at[stage * 8 + hop * 4 + which * 2 + way])

    both = [(which, way) for which in range(2) for way in range(2)]

    def core_copy(i, ref):
        copy = rcopy(ref, ref, core_s.at[i], core_r.at[i], page, sibling)
        copy.start()
        return copy

    wait_recv(w.at[c, x, pl.ds(0, NZ - 1), yh, yl], z_r)
    for which, way in both:
        ring_copy(0, which, 0, way).start()
    for which, way in both:
        ring_arrived(0, which, 0, way)
        ring_copy(0, which, 1, way).start()

    own_first.wait()
    wait_recv(frecv.at[pl.ds(0, TOKS - 1)], tok_r)

    @pl.loop(0, 4)
    def _(r):
        rows = pl.ds(pl.multiple_of(r * 128, 128), 128)
        second = matmul(psel[rows, :], frecv[...].reshape(ROWS, D))
        mixed = (pre[rows, :].astype(F32) + second).astype(BF)
        p1tx[pl.ds(r * 8, 8)] = mixed.reshape(8, PER, D)

    @pl.loop(1, PAGES)
    def _(k):
        to = mod(page + k, PAGES)
        rcopy(p1tx.at[to], p1rx.at[page], p1_s, p1_r, to, tok).start()

    own_p1 = pltpu.make_async_copy(p1tx.at[page], p1rx.at[page], own_s.at[1])
    own_p1.start()

    for which, way in both:
        ring_arrived(0, which, 1, way)
    for which, way in both:
        ring_copy(1, which, 0, way).start()
    cores = [core_copy(0, ylo(y, 0, 4)), core_copy(1, xhi(x, 4, 4))]
    for which, way in both:
        ring_arrived(1, which, 0, way)
        ring_copy(1, which, 1, way).start()
        piece, me, dev, z0, n = rings[1][which]
        by = 1 if way == 0 else n - 1
        cores.append(core_copy(2 + 2 * which + way, piece(mod(me + n - by, n), z0, 4)))

    own_p1.wait()
    wait_recv(p1rx.at[pl.ds(0, PAGES - 1)], p1_r)

    @pl.loop(0, 4)
    def _(r):
        rows = pl.ds(pl.multiple_of(r * 128, 128), 128)
        row = iota((128, ROWS), 0) + r * 128
        col = iota((128, ROWS), 1)
        target = (row // PER) * ROWS + page * PER + row % PER
        pick = (row % PER == col % PER) & (target >= start_of) & (target < stop_of)
        mixed = matmul(pick.astype(BF), p1rx[...].reshape(ROWS, D))
        ymix[rows, :] = mixed.astype(BF)
        ynorm[rows, :] = rms_round(mixed)

    for which, way in both:
        ring_arrived(1, which, 1, way)
    cores.append(core_copy(6, ylo(mod(y + 2, NY), 0, 4)))
    cores.append(core_copy(7, xhi(mod(x + 2, NX), 4, 4)))
    for copy in cores:
        copy.wait_recv()

    @pl.loop(0, 8)
    def _(t):
        at = (t // 2, pl.ds(4 * (t % 2), 4))
        gate = matmul_nt(ynorm[...], w[(0, *at, slice(None), slice(None), slice(None), slice(0, D))].reshape(256, D))
        up = matmul_nt(ynorm[...], w[(1, *at, slice(None), slice(None), slice(None), slice(0, D))].reshape(256, D))
        hid[:, pl.ds(pl.multiple_of(t * 256, 256), 256)] = (gate / (1.0 + jnp.exp(-gate)) * up).astype(BF)

    @pl.loop(0, 4)
    def _(t):
        cols = pl.ds(pl.multiple_of(t * 256, 256), 256)
        total = ymix[:, cols].astype(F32)
        for q in range(4):
            down = w[q % 2, t, :, :, q // 2, :, D:].reshape(256, 512)
            total = total + matmul_nt(hid[:, q * 512 : (q + 1) * 512], down)
        p2tx[:, :, cols] = total.astype(BF).reshape(PAGES, PER, 256)

    @pl.loop(1, PAGES)
    def _(k):
        to = mod(page + k, PAGES)
        rcopy(p2tx.at[to], o_ref.at[page], p2_s, p2_r, to, tok).start()

    own_p2 = pltpu.make_async_copy(p2tx.at[page], o_ref.at[page], own_s.at[2])
    own_p2.start()

    wait_send(gu_rx, gu_s)
    wait_send(wd_rx, wd_s)
    wait_send(lens_rx.at[pl.ds(0, PAGES - 1)], lens_s)
    wait_send(w.at[c, x, pl.ds(0, NZ - 1), yh, yl], z_s)
    wait_send(frecv.at[pl.ds(0, TOKS - 1)], tok_s)
    wait_send(p1tx.at[pl.ds(0, PAGES - 1)], p1_s)
    for stage in range(2):
        for hop in range(2):
            for which, way in both:
                ring_copy(stage, which, hop, way).wait_send()
    for copy in cores:
        copy.wait_send()
    own_p2.wait()
    wait_send(p2tx.at[pl.ds(0, PAGES - 1)], p2_s)
    wait_recv(o_ref.at[pl.ds(0, PAGES - 1)], p2_r)


def per_device(tile_tokens, page_lengths, occupancy, block_mix, stride_mix, w_gate_up, w_down):
    vmem = pl.BlockSpec(memory_space=pltpu.VMEM)
    smem = pl.BlockSpec(memory_space=pltpu.SMEM)
    dma = pltpu.SemaphoreType.DMA
    packed = pl.pallas_call(
        body,
        out_shape=jax.ShapeDtypeStruct((PAGES, PER, D), BF),
        in_specs=[smem, smem] + [vmem] * 5,
        out_specs=vmem,
        scratch_shapes=[
            pltpu.VMEM((PAGES, 8, 128), jnp.int32),
            pltpu.VMEM((2, 16, D), BF),
            pltpu.VMEM((16, D), BF),
            pltpu.VMEM((4, 16, 512), BF),
            pltpu.VMEM((3, 16, 512), BF),
            pltpu.VMEM((NC, NX, NZ, 2, 2, 16, D + 512), BF),
            pltpu.VMEM((TOKS, 4, PER, D), BF),
            pltpu.VMEM((TOKS, 4, PER, D), BF),
            pltpu.VMEM((ROWS, D), BF),
            pltpu.VMEM((ROWS, ROWS), BF),
            pltpu.VMEM((ROWS, D), BF),
            pltpu.VMEM((ROWS, ROWS), BF),
            pltpu.VMEM((PAGES, PER, D), BF),
            pltpu.VMEM((PAGES, PER, D), BF),
            pltpu.VMEM((ROWS, D), BF),
            pltpu.VMEM((ROWS, D), BF),
            pltpu.VMEM((ROWS, FF), BF),
            pltpu.VMEM((PAGES, PER, D), BF),
        ]
        + [dma] * 14
        + [dma((16,)), dma((16,)), dma((8,)), dma((8,)), dma((3,))],
        compiler_params=pltpu.CompilerParams(
            collective_id=0, has_side_effects=True, vmem_limit_bytes=48 * 1024 * 1024
        ),
    )(
        page_lengths, occupancy, tile_tokens[0], block_mix, stride_mix,
        jnp.swapaxes(w_gate_up, 1, 2), w_down.T,
    )
    return packed.reshape(1, ROWS, D)


def solution(mesh):
    return jax.shard_map(
        per_device,
        mesh=mesh,
        in_specs=(
            P("page", "tok", None),
            P("page"),
            P("page", "tok"),
            P("tok", None, None),
            P("tok", None, None),
            P(None, None, ("page", "tok")),
            P(None, ("page", "tok")),
        ),
        out_specs=P("tok", "page", None),
        check_vma=False,
    )
```

```python
import jax
import jax.numpy as jnp
from jax import lax
from jax.experimental import pallas as pl
from jax.experimental.pallas import tpu as pltpu
from jax.sharding import PartitionSpec as P

NX, NZ, NY, NC = 4, 8, 4, 2
PAGES, TOKS = 32, 8
ROWS, D, FF = 512, 1024, 2048
BLK, NB, PER = 128, 32, 16
EPS = 1e-05
SPLIT = 5
HALF = D // 2
MESH = pl.DeviceIdType.MESH
NT = (((1,), (1,)), ((), ()))
BF, F32 = jnp.bfloat16, jnp.float32


def mod(a, n):
    return lax.rem(a, jnp.int32(n))


def div(a, n):
    return lax.div(a, jnp.int32(n))


def iota(shape, dim):
    return lax.broadcasted_iota(jnp.int32, shape, dim)


def matmul(a, b):
    return jnp.dot(a, b, preferred_element_type=F32)


def matmul_nt(a, b):
    return lax.dot_general(a, b, NT, preferred_element_type=F32)


def rms_round(values):
    scale = lax.rsqrt(jnp.mean(values * values, axis=-1, keepdims=True) + EPS)
    return (values * scale).astype(BF)


def body(
    len_ref, occ_ref, x_hbm, bm_hbm, sm_hbm, wg_hbm, wd_hbm, o_ref,
    x_ref, bm_ref, sm_ref, wg_ref, wd_ref,
    lens_rx, gu_tx, gu_rx, wd_tx, wd_rx, zunit_gu, zunit_wd, gu_lo, gu_hi, wd_lo, wd_hi, fsend, frecv, xm, spread, pre, psel,
    p1tx, p1rx, ynorm, hid, p2tx, p2rx,
    lens_s, lens_r, gu_s, gu_r, wd_s, wd_r, z_s, z_r, tok_s, tok_r,
    p1_s, p1_r, p2_s, p2_r, ring_s, ring_r, core_s, core_r, own_s, in_s, keep_s,
):
    page, tok = lax.axis_index("page"), lax.axis_index("tok")
    x, z = div(page, NZ), mod(page, NZ)
    y, c = div(tok, NC), mod(tok, NC)
    yh, yl = div(y, 2), mod(y, 2)
    sibling = tok + 1 - 2 * c

    def rcopy(src, dst, ssem, rsem, to_page, to_tok):
        return pltpu.make_async_remote_copy(
            src_ref=src, dst_ref=dst, send_sem=ssem, recv_sem=rsem,
            device_id=(to_page, to_tok), device_id_type=MESH,
        )

    def wait_recv(ref, sem):
        rcopy(ref, ref, sem, sem, page, sibling).wait_recv()

    def wait_send(ref, sem):
        rcopy(ref, ref, sem, sem, page, sibling).wait_send()

    loads = [
        pltpu.make_async_copy(src, dst, in_s.at[i])
        for i, (src, dst) in enumerate(
            [(wg_hbm, wg_ref), (wd_hbm, wd_ref), (x_hbm, x_ref), (bm_hbm, bm_ref), (sm_hbm, sm_ref)]
        )
    ]
    for load in loads:
        load.start()
    barrier = pltpu.get_barrier_semaphore()

    @pl.loop(1, PAGES)
    def _(k):
        pl.semaphore_signal(barrier, inc=1, device_id=(mod(page + k, PAGES), tok), device_id_type=MESH)

    @pl.loop(1, TOKS)
    def _(k):
        pl.semaphore_signal(barrier, inc=1, device_id=(page, mod(tok + k, TOKS)), device_id_type=MESH)

    length = len_ref[0]
    loads[0].wait()
    loads[1].wait()
    place8 = (iota((16, 8), 0) == iota((16, 8), 1) + 8 * c).astype(BF)
    place4 = (iota((16, 4), 0) == iota((16, 4), 1) + 4 * mod(tok, 4)).astype(BF)
    for g in range(2):
        gu_tx[g] = matmul(place8, wg_ref[g]).astype(BF)
    wd_all = matmul(place4, wd_ref[...]).astype(BF)
    for q in range(4):
        wd_tx[q] = wd_all[:, q * 512 : (q + 1) * 512]
    lens_rx[page] = jnp.full((8, 128), length, jnp.int32)

    pl.semaphore_wait(barrier, PAGES - 1 + TOKS - 1)

    rcopy(gu_tx.at[1 - c], gu_rx, gu_s, gu_r, page, sibling).start()
    half = 4 * div(tok, 4)
    for k in range(1, 4):
        q = mod(tok + k, 4)
        rcopy(wd_tx.at[q], wd_rx.at[3 - k], wd_s, wd_r, page, half + q).start()

    loads[2].wait()
    loads[3].wait()
    for b in range(4):
        limit = length * occ_ref[0, b] - tok * ROWS - b * BLK
        rows = slice(b * BLK, (b + 1) * BLK)
        live = iota((BLK, D), 0) < limit
        masked = jnp.where(live, x_ref[rows, :].astype(F32), 0.0)
        xm[rows, :] = masked.astype(BF)
        first = matmul(bm_ref[b], rms_round(masked)).astype(BF)
        for h in range(2):
            fsend[h, :, b] = first[:, h * HALF : (h + 1) * HALF].reshape(TOKS, PER, HALF)

    own = []
    for h in range(2):
        own.append(pltpu.make_async_copy(fsend.at[h, tok], frecv.at[h, tok], own_s.at[h]))
        own[h].start()

        @pl.loop(1, TOKS)
        def _(k):
            to = mod(tok + k, TOKS)
            rcopy(fsend.at[h, to], frecv.at[h, tok], tok_s.at[h], tok_r.at[h], page, to).start()

    wait_recv(gu_rx, gu_r)
    wait_recv(wd_rx, wd_r)
    zunit_gu[z] = gu_tx[c] + gu_rx[...]
    zunit_wd[z] = wd_tx[mod(tok, 4)] + wd_rx[0] + wd_rx[1] + wd_rx[2]

    @pl.loop(1, NZ)
    def _(k):
        to = x * NZ + mod(z + k, NZ)
        rcopy(zunit_gu.at[z], zunit_gu.at[z], z_s.at[0], z_r.at[0], to, tok).start()
        rcopy(zunit_wd.at[z], zunit_wd.at[z], z_s.at[1], z_r.at[1], to, tok).start()

    @pl.loop(1, PAGES)
    def _(k):
        rcopy(lens_rx.at[page], lens_rx.at[page], lens_s, lens_r, mod(page + k, PAGES), tok).start()

    loads[4].wait()
    expand = (iota((NB, ROWS), 0) == iota((NB, ROWS), 1) >> 4).astype(BF)
    wide = matmul(sm_ref[...].reshape(ROWS, NB), expand)
    same = (iota((ROWS, ROWS), 1) & 15) == (iota((ROWS, ROWS), 0) >> 5)
    spread[...] = jnp.where(same, wide, 0.0).astype(BF)

    wait_recv(lens_rx.at[pl.ds(0, PAGES - 1)], lens_r)
    lens = lens_rx[:, 0, :]
    lens = jnp.concatenate([lens] * 4, axis=1)
    kept = jnp.clip(lens - tok * ROWS, 0, ROWS)
    who = iota((PAGES, ROWS), 0)
    lane_page = iota((PAGES, ROWS), 1) >> 4
    shift = jnp.sum(jnp.where(who < page, kept, 0), axis=0, keepdims=True)
    start_of = jnp.sum(jnp.where(who < lane_page, kept, 0), axis=0, keepdims=True)
    stop_of = start_of + jnp.sum(jnp.where(who == lane_page, kept, 0), axis=0, keepdims=True)

    @pl.loop(0, 4)
    def _(r):
        rows = pl.ds(pl.multiple_of(r * 128, 128), 128)
        slot = iota((128, ROWS), 0) + r * 128
        turn = (((iota((128, ROWS), 1) + shift) & (ROWS - 1)) == slot).astype(BF)
        pre[rows, :] = matmul(turn, xm[...]).astype(BF)
        psel[rows, :] = matmul(turn, spread[...]).astype(BF)

    los, his, zunits = [gu_lo, wd_lo], [gu_hi, wd_hi], [zunit_gu, zunit_wd]
    mid = (NZ - SPLIT + 1) // 2

    def xlo(xx, cut, kind):
        zs = [pl.ds(0, SPLIT), pl.ds(0, SPLIT // 2), pl.ds(SPLIT // 2, SPLIT - SPLIT // 2)][cut]
        return los[kind].at[c, yh, yl, xx, zs]

    def yhi(yy, cut, kind):
        zs = [pl.ds(0, NZ - SPLIT), pl.ds(0, mid), pl.ds(mid, NZ - SPLIT - mid)][cut]
        return his[kind].at[c, x, div(yy, 2), mod(yy, 2), zs]

    def ylo(yy, cut, kind):
        xs = [pl.ds(0, 4), pl.ds(0, 2), pl.ds(2, 2)][cut]
        return los[kind].at[c, div(yy, 2), mod(yy, 2), xs]

    def xhi(xx, cut, kind):
        ys = [pl.ds(0, 2), pl.ds(0, 1), pl.ds(1, 1)][cut]
        return his[kind].at[c, xx, ys]

    def xdev(by):
        return mod(x + by, NX) * NZ + z, tok

    def ydev(by):
        return page, mod(y + by, NY) * NC + c

    rings = [[(xlo, x, xdev), (yhi, y, ydev)], [(ylo, y, ydev), (xhi, x, xdev)]]

    def ring_copy(stage, kind, hop, which, way):
        piece, me, dev = rings[stage][which]
        by = 1 if way == 0 else 3
        ref = piece(me, 0, kind) if hop == 0 else piece(mod(me + 4 - by, 4), 1 + way, kind)
        src = ref
        if stage == 0 and hop == 0:
            src = zunits[kind].at[pl.ds(0, SPLIT) if which == 0 else pl.ds(SPLIT, NZ - SPLIT)]
        i = stage * 16 + kind * 8 + hop * 4 + which * 2 + way
        return rcopy(src, ref, ring_s.at[i], ring_r.at[i], *dev(by))

    def arriving(stage, kind, hop, which, way):
        piece, me, dev = rings[stage][which]
        by = 1 if way == 0 else 3
        return piece(mod(me + 4 - by, 4), 0, kind) if hop == 0 else piece(mod(me + 2, 4), 1 + way, kind)

    def ring_arrived(stage, kind, hop, which, way):
        i = stage * 16 + kind * 8 + hop * 4 + which * 2 + way
        wait_recv(arriving(stage, kind, hop, which, way), ring_r.at[i])

    both = [(which, way) for which in range(2) for way in range(2)]

    def core_copy(i, ref):
        copy = rcopy(ref, ref, core_s.at[i], core_r.at[i], page, sibling)
        copy.start()
        return copy

    for h in range(2):
        own[h].wait()
        wait_recv(frecv.at[h, pl.ds(0, TOKS - 1)], tok_r.at[h])

        @pl.loop(0, 4)
        def _(r):
            rows = pl.ds(pl.multiple_of(r * 128, 128), 128)
            second = matmul(psel[rows, :], frecv[h].reshape(ROWS, HALF))
            mixed = (pre[rows, h * HALF : (h + 1) * HALF].astype(F32) + second).astype(BF)
            p1tx[h, pl.ds(r * 8, 8)] = mixed.reshape(8, PER, HALF)

        @pl.loop(1, PAGES)
        def _(k):
            to = mod(page + k, PAGES)
            rcopy(p1tx.at[h, to], p1rx.at[h, page], p1_s.at[h], p1_r.at[h], to, tok).start()

        own.append(pltpu.make_async_copy(p1tx.at[h, page], p1rx.at[h, page], own_s.at[2 + h]))
        own[2 + h].start()

    keeps = []
    for kind in range(2):
        wait_recv(zunits[kind].at[pl.ds(0, NZ - 1)], z_r.at[kind])
        for which, way in both:
            ring_copy(0, kind, 0, which, way).start()
        for which in range(2):
            piece, me, dev = rings[0][which]
            span = pl.ds(0, SPLIT) if which == 0 else pl.ds(SPLIT, NZ - SPLIT)
            copy = pltpu.make_async_copy(zunits[kind].at[span], piece(me, 0, kind), keep_s.at[kind * 2 + which])
            copy.start()
            keeps.append(copy)
    for kind in range(2):
        for which, way in both:
            ring_arrived(0, kind, 0, which, way)
            ring_copy(0, kind, 1, which, way).start()
    for copy in keeps:
        copy.wait()
    cores = [[], []]
    for kind in range(2):
        for which, way in both:
            ring_arrived(0, kind, 1, which, way)
        for which, way in both:
            ring_copy(1, kind, 0, which, way).start()
    for kind in range(2):
        for which in range(2):
            piece, me, dev = rings[1][which]
            cores[kind].append(core_copy(kind * 10 + which, piece(me, 0, kind)))

    for h in range(2):
        own[2 + h].wait()
        wait_recv(p1rx.at[h, pl.ds(0, PAGES - 1)], p1_r.at[h])

        @pl.loop(0, 4)
        def _(r):
            row = iota((128, ROWS), 0) + r * 128
            col = iota((128, ROWS), 1)
            target = (row >> 4) * ROWS + page * PER + (row & 15)
            pick = ((row & 15) == (col & 15)) & (target >= start_of) & (target < stop_of)
            mixed = matmul(pick.astype(BF), p1rx[h].reshape(ROWS, HALF))
            p2tx[h, pl.ds(r * 8, 8)] = mixed.astype(BF).reshape(8, PER, HALF)

        @pl.loop(1, PAGES)
        def _(k):
            to = mod(page + k, PAGES)
            rcopy(p2tx.at[h, to], p2rx.at[h, page], p2_s.at[h], p2_r.at[h], to, tok).start()

        own.append(pltpu.make_async_copy(p2tx.at[h, page], p2rx.at[h, page], own_s.at[4 + h]))
        own[4 + h].start()
        for which, way in both:
            ring_arrived(1, h, 0, which, way)
            ring_copy(1, h, 1, which, way).start()
            cores[h].append(core_copy(h * 10 + 2 + which * 2 + way, arriving(1, h, 0, which, way)))

    def last_hop(kind):
        for which, way in both:
            ring_arrived(1, kind, 1, which, way)
            cores[kind].append(core_copy(kind * 10 + 6 + which * 2 + way, arriving(1, kind, 1, which, way)))

    last_hop(0)

    for h in range(2):
        own[4 + h].wait()
        wait_recv(p2rx.at[h, pl.ds(0, PAGES - 1)], p2_r.at[h])

    @pl.loop(0, 4)
    def _(r):
        rows = pl.ds(pl.multiple_of(r * 128, 128), 128)
        mixed = [p2rx[h, pl.ds(r * 8, 8)].reshape(128, HALF).astype(F32) for h in range(2)]
        total = sum(jnp.sum(v * v, axis=-1, keepdims=True) for v in mixed)
        scale = lax.rsqrt(total / D + EPS)
        for h in range(2):
            ynorm[rows, h * HALF : (h + 1) * HALF] = (mixed[h] * scale).astype(BF)

    for copy in cores[0]:
        copy.wait_recv()

    def unit(kind, core, xx, zz, ys):
        if zz < SPLIT:
            return los[kind][core, :, ys, xx, zz]
        return his[kind][core, xx, :, ys, zz - SPLIT]

    @pl.loop(0, 4)
    def _(xx):
        for t in range(2):
            zs = range(4 * t, 4 * t + 4)
            rows = [
                jnp.concatenate([unit(0, core, xx, zz, slice(None)).reshape(64, D) for zz in zs], axis=0)
                for core in range(2)
            ]
            gate, up = matmul_nt(ynorm[...], rows[0]), matmul_nt(ynorm[...], rows[1])
            cols = pl.ds(pl.multiple_of(xx * 512 + t * 256, 256), 256)
            hid[:, cols] = (gate / (1.0 + jnp.exp(-gate)) * up).astype(BF)

    last_hop(1)
    for copy in cores[1]:
        copy.wait_recv()

    @pl.loop(0, 4)
    def _(t):
        half_cols = pl.ds(pl.multiple_of((t & 1) * 256, 256), 256)
        total = p2rx[t >> 1, :, :, half_cols].reshape(ROWS, 256).astype(F32)
        for q in range(4):
            down = jnp.concatenate([unit(1, q % 2, t, zz, q // 2).reshape(32, 512) for zz in range(NZ)], axis=0)
            total = total + matmul_nt(hid[:, q * 512 : (q + 1) * 512], down)
        o_ref[:, pl.ds(pl.multiple_of(t * 256, 256), 256)] = total.astype(BF)

    wait_send(gu_rx, gu_s)
    wait_send(wd_rx, wd_s)
    wait_send(lens_rx.at[pl.ds(0, PAGES - 1)], lens_s)
    for kind in range(2):
        wait_send(zunits[kind].at[pl.ds(0, NZ - 1)], z_s.at[kind])
    for h in range(2):
        wait_send(frecv.at[h, pl.ds(0, TOKS - 1)], tok_s.at[h])
        wait_send(p1tx.at[h, pl.ds(0, PAGES - 1)], p1_s.at[h])
        wait_send(p2tx.at[h, pl.ds(0, PAGES - 1)], p2_s.at[h])
    for stage in range(2):
        for kind in range(2):
            for hop in range(2):
                for which, way in both:
                    ring_copy(stage, kind, hop, which, way).wait_send()
    for copy in cores[0] + cores[1]:
        copy.wait_send()


def per_device(tile_tokens, page_lengths, occupancy, block_mix, stride_mix, w_gate_up, w_down):
    vmem = pl.BlockSpec(memory_space=pltpu.VMEM)
    smem = pl.BlockSpec(memory_space=pltpu.SMEM)
    dma = pltpu.SemaphoreType.DMA
    anywhere = pl.BlockSpec(memory_space=pltpu.HBM)
    packed = pl.pallas_call(
        body,
        out_shape=jax.ShapeDtypeStruct((ROWS, D), BF),
        in_specs=[smem, smem] + [anywhere] * 5,
        out_specs=vmem,
        scratch_shapes=[
            pltpu.VMEM((ROWS, D), BF),
            pltpu.VMEM((4, BLK, BLK), BF),
            pltpu.VMEM((PER, NB, NB), BF),
            pltpu.VMEM((2, 8, D), BF),
            pltpu.VMEM((4, FF), BF),
            pltpu.VMEM((PAGES, 8, 128), jnp.int32),
            pltpu.VMEM((2, 16, D), BF),
            pltpu.VMEM((16, D), BF),
            pltpu.VMEM((4, 16, 512), BF),
            pltpu.VMEM((3, 16, 512), BF),
            pltpu.VMEM((NZ, 16, D), BF),
            pltpu.VMEM((NZ, 16, 512), BF),
            pltpu.VMEM((NC, 2, 2, NX, SPLIT, 16, D), BF),
            pltpu.VMEM((NC, NX, 2, 2, NZ - SPLIT, 16, D), BF),
            pltpu.VMEM((NC, 2, 2, NX, SPLIT, 16, 512), BF),
            pltpu.VMEM((NC, NX, 2, 2, NZ - SPLIT, 16, 512), BF),
            pltpu.VMEM((2, TOKS, 4, PER, HALF), BF),
            pltpu.VMEM((2, TOKS, 4, PER, HALF), BF),
            pltpu.VMEM((ROWS, D), BF),
            pltpu.VMEM((ROWS, ROWS), BF),
            pltpu.VMEM((ROWS, D), BF),
            pltpu.VMEM((ROWS, ROWS), BF),
            pltpu.VMEM((2, PAGES, PER, HALF), BF),
            pltpu.VMEM((2, PAGES, PER, HALF), BF),
            pltpu.VMEM((ROWS, D), BF),
            pltpu.VMEM((ROWS, FF), BF),
            pltpu.VMEM((2, PAGES, PER, HALF), BF),
            pltpu.VMEM((2, PAGES, PER, HALF), BF),
        ]
        + [dma] * 6
        + [dma((2,))] * 8
        + [dma((32,)), dma((32,)), dma((20,)), dma((20,)), dma((6,)), dma((5,)), dma((4,))],
        compiler_params=pltpu.CompilerParams(
            collective_id=0, has_side_effects=True, vmem_limit_bytes=62 * 1024 * 1024
        ),
    )(
        page_lengths, occupancy, tile_tokens[0], block_mix, stride_mix,
        jnp.swapaxes(w_gate_up, 1, 2), w_down.T,
    )
    return packed.reshape(1, ROWS, D)


def solution(mesh):
    return jax.shard_map(
        per_device,
        mesh=mesh,
        in_specs=(
            P("page", "tok", None),
            P("page"),
            P("page", "tok"),
            P("tok", None, None),
            P("tok", None, None),
            P(None, None, ("page", "tok")),
            P(None, ("page", "tok")),
        ),
        out_specs=P("tok", "page", None),
        check_vma=False,
    )
```

```python
import jax
import jax.numpy as jnp
from jax import lax
from jax.experimental import pallas as pl
from jax.experimental.pallas import tpu as pltpu
from jax.sharding import PartitionSpec as P

NX, NZ, NY, NC = 4, 8, 4, 2
PAGES, TOKS = 32, 8
ROWS, D, FF = 512, 1024, 2048
BLK, NB, PER = 128, 32, 16
EPS = 1e-05
SPLIT = 5
HALF = D // 2
MESH = pl.DeviceIdType.MESH
NT = (((1,), (1,)), ((), ()))
BF, F32 = jnp.bfloat16, jnp.float32


def mod(a, n):
    return lax.rem(a, jnp.int32(n))


def div(a, n):
    return lax.div(a, jnp.int32(n))


def iota(shape, dim):
    return lax.broadcasted_iota(jnp.int32, shape, dim)


def matmul(a, b):
    return jnp.dot(a, b, preferred_element_type=F32)


def matmul_nt(a, b):
    return lax.dot_general(a, b, NT, preferred_element_type=F32)


def rms_round(values):
    scale = lax.rsqrt(jnp.mean(values * values, axis=-1, keepdims=True) + EPS)
    return (values * scale).astype(BF)


def body(
    len_ref, occ_ref, x_hbm, bm_hbm, sm_hbm, wg_hbm, wd_hbm, o_ref,
    x_ref, bm_ref, sm_ref, wg_ref, wd_ref,
    lens_rx, gu_tx, gu_rx, wd_tx, wd_rx, zunit_gu, zunit_wd, gu_lo, gu_hi, wd_lo, wd_hi, fsend, frecv, xm, spread, pre, psel,
    p1tx, p1rx, ynorm, hid, p2tx, p2rx,
    lens_s, lens_r, gu_s, gu_r, wd_s, wd_r, z_s, z_r, tok_s, tok_r,
    p1_s, p1_r, p2_s, p2_r, ring_s, ring_r, core_s, core_r, own_s, in_s, keep_s,
):
    page, tok = lax.axis_index("page"), lax.axis_index("tok")
    x, z = div(page, NZ), mod(page, NZ)
    y, c = div(tok, NC), mod(tok, NC)
    yh, yl = div(y, 2), mod(y, 2)
    sibling = tok + 1 - 2 * c

    def rcopy(src, dst, ssem, rsem, to_page, to_tok):
        return pltpu.make_async_remote_copy(
            src_ref=src, dst_ref=dst, send_sem=ssem, recv_sem=rsem,
            device_id=(to_page, to_tok), device_id_type=MESH,
        )

    def wait_recv(ref, sem):
        rcopy(ref, ref, sem, sem, page, sibling).wait_recv()

    def wait_send(ref, sem):
        rcopy(ref, ref, sem, sem, page, sibling).wait_send()

    loads = [
        pltpu.make_async_copy(src, dst, in_s.at[i])
        for i, (src, dst) in enumerate(
            [(wg_hbm, wg_ref), (wd_hbm, wd_ref), (x_hbm, x_ref), (bm_hbm, bm_ref), (sm_hbm, sm_ref)]
        )
    ]
    for load in loads:
        load.start()
    barrier = pltpu.get_barrier_semaphore()

    @pl.loop(1, PAGES)
    def _(k):
        pl.semaphore_signal(barrier, inc=1, device_id=(mod(page + k, PAGES), tok), device_id_type=MESH)

    @pl.loop(1, TOKS)
    def _(k):
        pl.semaphore_signal(barrier, inc=1, device_id=(page, mod(tok + k, TOKS)), device_id_type=MESH)

    length = len_ref[0]
    loads[0].wait()
    loads[1].wait()
    place8 = (iota((16, 8), 0) == iota((16, 8), 1) + 8 * c).astype(BF)
    place4 = (iota((16, 4), 0) == iota((16, 4), 1) + 4 * mod(tok, 4)).astype(BF)
    for g in range(2):
        gu_tx[g] = matmul(place8, wg_ref[g]).astype(BF)
    wd_all = matmul(place4, wd_ref[...]).astype(BF)
    for q in range(4):
        wd_tx[q] = wd_all[:, q * 512 : (q + 1) * 512]
    lens_rx[page] = jnp.full((1, 128), length, jnp.int32)

    loads[2].wait()
    loads[3].wait()
    for b in range(4):
        limit = length * occ_ref[0, b] - tok * ROWS - b * BLK
        rows = slice(b * BLK, (b + 1) * BLK)
        live = iota((BLK, D), 0) < limit
        masked = jnp.where(live, x_ref[rows, :].astype(F32), 0.0)
        xm[rows, :] = masked.astype(BF)
        first = matmul(bm_ref[b], rms_round(masked)).astype(BF)
        for h in range(2):
            fsend[h, :, b] = first[:, h * HALF : (h + 1) * HALF].reshape(TOKS, PER, HALF)

    pl.semaphore_wait(barrier, PAGES - 1 + TOKS - 1)

    rcopy(gu_tx.at[1 - c], gu_rx, gu_s, gu_r, page, sibling).start()
    half = 4 * div(tok, 4)
    for k in range(1, 4):
        q = mod(tok + k, 4)
        rcopy(wd_tx.at[q], wd_rx.at[3 - k], wd_s, wd_r, page, half + q).start()

    own = []

    def send_first(h):
        own.append(pltpu.make_async_copy(fsend.at[h, tok], frecv.at[h, tok], own_s.at[h]))
        own[h].start()

        @pl.loop(1, TOKS)
        def _(k):
            to = mod(tok + k, TOKS)
            rcopy(fsend.at[h, to], frecv.at[h, tok], tok_s.at[h], tok_r.at[h], page, to).start()

    send_first(0)

    @pl.loop(1, PAGES)
    def _(k):
        rcopy(lens_rx.at[page], lens_rx.at[page], lens_s, lens_r, mod(page + k, PAGES), tok).start()

    send_first(1)

    wait_recv(gu_rx, gu_r)
    wait_recv(wd_rx, wd_r)
    zunit_gu[z] = gu_tx[c] + gu_rx[...]
    zunit_wd[z] = wd_tx[mod(tok, 4)] + wd_rx[0] + wd_rx[1] + wd_rx[2]

    @pl.loop(1, NZ)
    def _(k):
        to = x * NZ + mod(z + k, NZ)
        rcopy(zunit_gu.at[z], zunit_gu.at[z], z_s.at[0], z_r.at[0], to, tok).start()
        rcopy(zunit_wd.at[z], zunit_wd.at[z], z_s.at[1], z_r.at[1], to, tok).start()

    loads[4].wait()
    expand = (iota((NB, ROWS), 0) == iota((NB, ROWS), 1) >> 4).astype(BF)
    wide = matmul(sm_ref[...].reshape(ROWS, NB), expand)
    same = (iota((ROWS, ROWS), 1) & 15) == (iota((ROWS, ROWS), 0) >> 5)
    spread[...] = jnp.where(same, wide, 0.0).astype(BF)

    wait_recv(lens_rx.at[pl.ds(0, PAGES - 1)], lens_r)
    lens = lens_rx[:, 0, :]
    lens = jnp.concatenate([lens] * 4, axis=1)
    kept = jnp.clip(lens - tok * ROWS, 0, ROWS)
    who = iota((PAGES, ROWS), 0)
    lane_page = iota((PAGES, ROWS), 1) >> 4
    shift = jnp.sum(jnp.where(who < page, kept, 0), axis=0, keepdims=True)
    start_of = jnp.sum(jnp.where(who < lane_page, kept, 0), axis=0, keepdims=True)
    stop_of = start_of + jnp.sum(jnp.where(who == lane_page, kept, 0), axis=0, keepdims=True)

    @pl.loop(0, 4)
    def _(r):
        rows = pl.ds(pl.multiple_of(r * 128, 128), 128)
        slot = iota((128, ROWS), 0) + r * 128
        turn = (((iota((128, ROWS), 1) + shift) & (ROWS - 1)) == slot).astype(BF)
        pre[rows, :] = matmul(turn, xm[...]).astype(BF)
        psel[rows, :] = matmul(turn, spread[...]).astype(BF)

    los, his, zunits = [gu_lo, wd_lo], [gu_hi, wd_hi], [zunit_gu, zunit_wd]
    mid = (NZ - SPLIT + 1) // 2

    def xlo(xx, cut, kind):
        zs = [pl.ds(0, SPLIT), pl.ds(0, SPLIT // 2), pl.ds(SPLIT // 2, SPLIT - SPLIT // 2)][cut]
        return los[kind].at[c, yh, yl, xx, zs]

    def yhi(yy, cut, kind):
        zs = [pl.ds(0, NZ - SPLIT), pl.ds(0, mid), pl.ds(mid, NZ - SPLIT - mid)][cut]
        return his[kind].at[c, x, div(yy, 2), mod(yy, 2), zs]

    def ylo(yy, cut, kind):
        xs = [pl.ds(0, 4), pl.ds(0, 2), pl.ds(2, 2)][cut]
        return los[kind].at[c, div(yy, 2), mod(yy, 2), xs]

    def xhi(xx, cut, kind):
        ys = [pl.ds(0, 2), pl.ds(0, 1), pl.ds(1, 1)][cut]
        return his[kind].at[c, xx, ys]

    def xdev(by):
        return mod(x + by, NX) * NZ + z, tok

    def ydev(by):
        return page, mod(y + by, NY) * NC + c

    rings = [[(xlo, x, xdev), (yhi, y, ydev)], [(ylo, y, ydev), (xhi, x, xdev)]]

    def ring_copy(stage, kind, hop, which, way):
        piece, me, dev = rings[stage][which]
        by = 1 if way == 0 else 3
        ref = piece(me, 0, kind) if hop == 0 else piece(mod(me + 4 - by, 4), 1 + way, kind)
        src = ref
        if stage == 0 and hop == 0:
            src = zunits[kind].at[pl.ds(0, SPLIT) if which == 0 else pl.ds(SPLIT, NZ - SPLIT)]
        i = stage * 16 + kind * 8 + hop * 4 + which * 2 + way
        return rcopy(src, ref, ring_s.at[i], ring_r.at[i], *dev(by))

    def arriving(stage, kind, hop, which, way):
        piece, me, dev = rings[stage][which]
        by = 1 if way == 0 else 3
        return piece(mod(me + 4 - by, 4), 0, kind) if hop == 0 else piece(mod(me + 2, 4), 1 + way, kind)

    def ring_arrived(stage, kind, hop, which, way):
        i = stage * 16 + kind * 8 + hop * 4 + which * 2 + way
        wait_recv(arriving(stage, kind, hop, which, way), ring_r.at[i])

    both = [(which, way) for which in range(2) for way in range(2)]

    def core_copy(i, ref):
        copy = rcopy(ref, ref, core_s.at[i], core_r.at[i], page, sibling)
        copy.start()
        return copy

    for h in range(2):
        own[h].wait()
        wait_recv(frecv.at[h, pl.ds(0, TOKS - 1)], tok_r.at[h])

        @pl.loop(0, 4)
        def _(r):
            rows = pl.ds(pl.multiple_of(r * 128, 128), 128)
            second = matmul(psel[rows, :], frecv[h].reshape(ROWS, HALF))
            mixed = (pre[rows, h * HALF : (h + 1) * HALF].astype(F32) + second).astype(BF)
            p1tx[h, pl.ds(r * 8, 8)] = mixed.reshape(8, PER, HALF)

        @pl.loop(1, PAGES)
        def _(k):
            to = mod(page + k, PAGES)
            rcopy(p1tx.at[h, to], p1rx.at[h, page], p1_s.at[h], p1_r.at[h], to, tok).start()

        own.append(pltpu.make_async_copy(p1tx.at[h, page], p1rx.at[h, page], own_s.at[2 + h]))
        own[2 + h].start()

    keeps = []
    for kind in range(2):
        wait_recv(zunits[kind].at[pl.ds(0, NZ - 1)], z_r.at[kind])
        for which, way in both:
            ring_copy(0, kind, 0, which, way).start()
        for which in range(2):
            piece, me, dev = rings[0][which]
            span = pl.ds(0, SPLIT) if which == 0 else pl.ds(SPLIT, NZ - SPLIT)
            copy = pltpu.make_async_copy(zunits[kind].at[span], piece(me, 0, kind), keep_s.at[kind * 2 + which])
            copy.start()
            keeps.append(copy)
    for kind in range(2):
        for which, way in both:
            ring_arrived(0, kind, 0, which, way)
            ring_copy(0, kind, 1, which, way).start()
    for copy in keeps:
        copy.wait()
    cores = [[], []]
    for kind in range(2):
        for which, way in both:
            ring_arrived(0, kind, 1, which, way)
        for which, way in both:
            ring_copy(1, kind, 0, which, way).start()
    for kind in range(2):
        for which in range(2):
            piece, me, dev = rings[1][which]
            cores[kind].append(core_copy(kind * 10 + which, piece(me, 0, kind)))

    for h in range(2):
        own[2 + h].wait()
        wait_recv(p1rx.at[h, pl.ds(0, PAGES - 1)], p1_r.at[h])

        @pl.loop(0, 4)
        def _(r):
            row = iota((128, ROWS), 0) + r * 128
            col = iota((128, ROWS), 1)
            target = (row >> 4) * ROWS + page * PER + (row & 15)
            pick = ((row & 15) == (col & 15)) & (target >= start_of) & (target < stop_of)
            mixed = matmul(pick.astype(BF), p1rx[h].reshape(ROWS, HALF))
            p2tx[h, pl.ds(r * 8, 8)] = mixed.astype(BF).reshape(8, PER, HALF)

        @pl.loop(1, PAGES)
        def _(k):
            to = mod(page + k, PAGES)
            rcopy(p2tx.at[h, to], p2rx.at[h, page], p2_s.at[h], p2_r.at[h], to, tok).start()

        own.append(pltpu.make_async_copy(p2tx.at[h, page], p2rx.at[h, page], own_s.at[4 + h]))
        own[4 + h].start()
        for which, way in both:
            ring_arrived(1, h, 0, which, way)
            ring_copy(1, h, 1, which, way).start()
            cores[h].append(core_copy(h * 10 + 2 + which * 2 + way, arriving(1, h, 0, which, way)))

    def last_hop(kind):
        for which, way in both:
            ring_arrived(1, kind, 1, which, way)
            cores[kind].append(core_copy(kind * 10 + 6 + which * 2 + way, arriving(1, kind, 1, which, way)))

    last_hop(0)

    for h in range(2):
        own[4 + h].wait()
        wait_recv(p2rx.at[h, pl.ds(0, PAGES - 1)], p2_r.at[h])

    @pl.loop(0, 4)
    def _(r):
        rows = pl.ds(pl.multiple_of(r * 128, 128), 128)
        mixed = [p2rx[h, pl.ds(r * 8, 8)].reshape(128, HALF).astype(F32) for h in range(2)]
        total = sum(jnp.sum(v * v, axis=-1, keepdims=True) for v in mixed)
        scale = lax.rsqrt(total / D + EPS)
        for h in range(2):
            ynorm[rows, h * HALF : (h + 1) * HALF] = (mixed[h] * scale).astype(BF)

    for copy in cores[0]:
        copy.wait_recv()

    def unit(kind, core, xx, zz, ys):
        if zz < SPLIT:
            return los[kind][core, :, ys, xx, zz]
        return his[kind][core, xx, :, ys, zz - SPLIT]

    @pl.loop(0, 4)
    def _(xx):
        for t in range(2):
            zs = range(4 * t, 4 * t + 4)
            rows = [
                jnp.concatenate([unit(0, core, xx, zz, slice(None)).reshape(64, D) for zz in zs], axis=0)
                for core in range(2)
            ]
            gate, up = matmul_nt(ynorm[...], rows[0]), matmul_nt(ynorm[...], rows[1])
            cols = pl.ds(pl.multiple_of(xx * 512 + t * 256, 256), 256)
            hid[:, cols] = (gate / (1.0 + jnp.exp(-gate)) * up).astype(BF)

    last_hop(1)
    for copy in cores[1]:
        copy.wait_recv()

    @pl.loop(0, 4)
    def _(t):
        half_cols = pl.ds(pl.multiple_of((t & 1) * 256, 256), 256)
        total = p2rx[t >> 1, :, :, half_cols].reshape(ROWS, 256).astype(F32)
        for q in range(4):
            down = jnp.concatenate([unit(1, q % 2, t, zz, q // 2).reshape(32, 512) for zz in range(NZ)], axis=0)
            total = total + matmul_nt(hid[:, q * 512 : (q + 1) * 512], down)
        o_ref[:, pl.ds(pl.multiple_of(t * 256, 256), 256)] = total.astype(BF)

    wait_send(gu_rx, gu_s)
    wait_send(wd_rx, wd_s)
    wait_send(lens_rx.at[pl.ds(0, PAGES - 1)], lens_s)
    for kind in range(2):
        wait_send(zunits[kind].at[pl.ds(0, NZ - 1)], z_s.at[kind])
    for h in range(2):
        wait_send(frecv.at[h, pl.ds(0, TOKS - 1)], tok_s.at[h])
        wait_send(p1tx.at[h, pl.ds(0, PAGES - 1)], p1_s.at[h])
        wait_send(p2tx.at[h, pl.ds(0, PAGES - 1)], p2_s.at[h])
    for stage in range(2):
        for kind in range(2):
            for hop in range(2):
                for which, way in both:
                    ring_copy(stage, kind, hop, which, way).wait_send()
    for copy in cores[0] + cores[1]:
        copy.wait_send()


def per_device(tile_tokens, page_lengths, occupancy, block_mix, stride_mix, w_gate_up, w_down):
    vmem = pl.BlockSpec(memory_space=pltpu.VMEM)
    smem = pl.BlockSpec(memory_space=pltpu.SMEM)
    dma = pltpu.SemaphoreType.DMA
    anywhere = pl.BlockSpec(memory_space=pltpu.HBM)
    packed = pl.pallas_call(
        body,
        out_shape=jax.ShapeDtypeStruct((ROWS, D), BF),
        in_specs=[smem, smem] + [anywhere] * 5,
        out_specs=vmem,
        scratch_shapes=[
            pltpu.VMEM((ROWS, D), BF),
            pltpu.VMEM((4, BLK, BLK), BF),
            pltpu.VMEM((PER, NB, NB), BF),
            pltpu.VMEM((2, 8, D), BF),
            pltpu.VMEM((4, FF), BF),
            pltpu.VMEM((PAGES, 1, 128), jnp.int32),
            pltpu.VMEM((2, 16, D), BF),
            pltpu.VMEM((16, D), BF),
            pltpu.VMEM((4, 16, 512), BF),
            pltpu.VMEM((3, 16, 512), BF),
            pltpu.VMEM((NZ, 16, D), BF),
            pltpu.VMEM((NZ, 16, 512), BF),
            pltpu.VMEM((NC, 2, 2, NX, SPLIT, 16, D), BF),
            pltpu.VMEM((NC, NX, 2, 2, NZ - SPLIT, 16, D), BF),
            pltpu.VMEM((NC, 2, 2, NX, SPLIT, 16, 512), BF),
            pltpu.VMEM((NC, NX, 2, 2, NZ - SPLIT, 16, 512), BF),
            pltpu.VMEM((2, TOKS, 4, PER, HALF), BF),
            pltpu.VMEM((2, TOKS, 4, PER, HALF), BF),
            pltpu.VMEM((ROWS, D), BF),
            pltpu.VMEM((ROWS, ROWS), BF),
            pltpu.VMEM((ROWS, D), BF),
            pltpu.VMEM((ROWS, ROWS), BF),
            pltpu.VMEM((2, PAGES, PER, HALF), BF),
            pltpu.VMEM((2, PAGES, PER, HALF), BF),
            pltpu.VMEM((ROWS, D), BF),
            pltpu.VMEM((ROWS, FF), BF),
            pltpu.VMEM((2, PAGES, PER, HALF), BF),
            pltpu.VMEM((2, PAGES, PER, HALF), BF),
        ]
        + [dma] * 6
        + [dma((2,))] * 8
        + [dma((32,)), dma((32,)), dma((20,)), dma((20,)), dma((6,)), dma((5,)), dma((4,))],
        compiler_params=pltpu.CompilerParams(
            collective_id=0, has_side_effects=True, vmem_limit_bytes=48 * 1024 * 1024
        ),
    )(
        page_lengths, occupancy,
        *(
            pltpu.with_memory_space_constraint(v, pltpu.HBM)
            for v in (tile_tokens[0], block_mix, stride_mix, jnp.swapaxes(w_gate_up, 1, 2), w_down.T)
        ),
    )
    return packed.reshape(1, ROWS, D)


def solution(mesh):
    return jax.shard_map(
        per_device,
        mesh=mesh,
        in_specs=(
            P("page", "tok", None),
            P("page"),
            P("page", "tok"),
            P("tok", None, None),
            P("tok", None, None),
            P(None, None, ("page", "tok")),
            P(None, ("page", "tok")),
        ),
        out_specs=P("tok", "page", None),
        check_vma=False,
    )
```

```python
import jax
import jax.numpy as jnp
from jax import lax
from jax.experimental import pallas as pl
from jax.experimental.pallas import tpu as pltpu
from jax.sharding import PartitionSpec as P

NX, NZ, NY, NC = 4, 8, 4, 2
PAGES, TOKS = 32, 8
ROWS, D, FF = 512, 1024, 2048
BLK, NB, PER = 128, 32, 16
EPS = 1e-05
SPLIT = 5
CHUNKS = ((0, 256), (256, 256), (512, 512))
MESH = pl.DeviceIdType.MESH
NT = (((1,), (1,)), ((), ()))
BF, F32 = jnp.bfloat16, jnp.float32


def mod(a, n):
    return lax.rem(a, jnp.int32(n))


def div(a, n):
    return lax.div(a, jnp.int32(n))


def iota(shape, dim):
    return lax.broadcasted_iota(jnp.int32, shape, dim)


def matmul(a, b):
    return jnp.dot(a, b, preferred_element_type=F32)


def matmul_nt(a, b):
    return lax.dot_general(a, b, NT, preferred_element_type=F32)


def rms_round(values):
    scale = lax.rsqrt(jnp.mean(values * values, axis=-1, keepdims=True) + EPS)
    return (values * scale).astype(BF)


def body(
    len_ref, occ_ref, x_hbm, bm_hbm, sm_hbm, wg_hbm, wd_hbm, o_ref,
    x_ref, bm_ref, sm_ref, wg_ref, wd_ref,
    lens_rx, gu_tx, gu_rx, wd_tx, wd_rx, zunit_gu, zunit_wd, gu_lo, gu_hi, wd_lo, wd_hi, xm, spread, pre, psel, picks,
    ynorm, hid,
    fsend, frecv, p1tx, p1rx, p2tx, p2rx,
    lens_s, lens_r, gu_s, gu_r, wd_s, wd_r, z_s, z_r, tok_s, tok_r,
    p1_s, p1_r, p2_s, p2_r, ring_s, ring_r, core_s, core_r, own_s, in_s, keep_s, z2_s, z2_r,
):
    page, tok = lax.axis_index("page"), lax.axis_index("tok")
    x, z = div(page, NZ), mod(page, NZ)
    y, c = div(tok, NC), mod(tok, NC)
    yh, yl = div(y, 2), mod(y, 2)
    sibling = tok + 1 - 2 * c

    def rcopy(src, dst, ssem, rsem, to_page, to_tok):
        return pltpu.make_async_remote_copy(
            src_ref=src, dst_ref=dst, send_sem=ssem, recv_sem=rsem,
            device_id=(to_page, to_tok), device_id_type=MESH,
        )

    def wait_recv(ref, sem):
        rcopy(ref, ref, sem, sem, page, sibling).wait_recv()

    def wait_send(ref, sem):
        rcopy(ref, ref, sem, sem, page, sibling).wait_send()

    loads = [
        pltpu.make_async_copy(src, dst, in_s.at[i])
        for i, (src, dst) in enumerate(
            [(wg_hbm, wg_ref), (wd_hbm, wd_ref), (x_hbm, x_ref), (bm_hbm, bm_ref), (sm_hbm, sm_ref)]
        )
    ]
    for load in loads:
        load.start()
    barrier = pltpu.get_barrier_semaphore()

    @pl.loop(1, PAGES)
    def _(k):
        pl.semaphore_signal(barrier, inc=1, device_id=(mod(page + k, PAGES), tok), device_id_type=MESH)

    @pl.loop(1, TOKS)
    def _(k):
        pl.semaphore_signal(barrier, inc=1, device_id=(page, mod(tok + k, TOKS)), device_id_type=MESH)

    length = len_ref[0]
    loads[0].wait()
    loads[1].wait()
    place8 = (iota((16, 8), 0) == iota((16, 8), 1) + 8 * c).astype(BF)
    place4 = (iota((16, 4), 0) == iota((16, 4), 1) + 4 * mod(tok, 4)).astype(BF)
    for g in range(2):
        gu_tx[g] = matmul(place8, wg_ref[g]).astype(BF)
    wd_all = matmul(place4, wd_ref[...]).astype(BF)
    for q in range(4):
        wd_tx[q] = wd_all[:, q * 512 : (q + 1) * 512]
    lens_rx[page] = jnp.full((1, 128), length, jnp.int32)

    loads[2].wait()
    loads[3].wait()
    for b in range(4):
        limit = length * occ_ref[0, b] - tok * ROWS - b * BLK
        rows = slice(b * BLK, (b + 1) * BLK)
        live = iota((BLK, D), 0) < limit
        masked = jnp.where(live, x_ref[rows, :].astype(F32), 0.0)
        xm[rows, :] = masked.astype(BF)
        first = matmul(bm_ref[b], rms_round(masked)).astype(BF)
        for h, (at, n) in enumerate(CHUNKS):
            fsend[h][:, b] = first[:, at : at + n].reshape(TOKS, PER, n)

    pl.semaphore_wait(barrier, PAGES - 1 + TOKS - 1)

    @pl.loop(1, PAGES)
    def _(k):
        rcopy(lens_rx.at[page], lens_rx.at[page], lens_s, lens_r, mod(page + k, PAGES), tok).start()

    rcopy(gu_tx.at[1 - c], gu_rx, gu_s, gu_r, page, sibling).start()
    half = 4 * div(tok, 4)
    for k in range(1, 4):
        q = mod(tok + k, 4)
        rcopy(wd_tx.at[q], wd_rx.at[3 - k], wd_s, wd_r, page, half + q).start()

    own = []
    for h in range(len(CHUNKS)):
        own.append(pltpu.make_async_copy(fsend[h].at[tok], frecv[h].at[tok], own_s.at[h]))
        own[h].start()

        @pl.loop(1, TOKS)
        def _(k):
            to = mod(tok + k, TOKS)
            rcopy(fsend[h].at[to], frecv[h].at[tok], tok_s.at[h], tok_r.at[h], page, to).start()

    wait_recv(gu_rx, gu_r)
    wait_recv(wd_rx, wd_r)
    zunit_gu[z] = gu_tx[c] + gu_rx[...]
    zunit_wd[z] = wd_tx[mod(tok, 4)] + wd_rx[0] + wd_rx[1] + wd_rx[2]
    zunits = [zunit_gu, zunit_wd]

    def z_copy(kind, origin, by, ssem, rsem):
        ref = zunits[kind].at[mod(z + origin + NZ, NZ)]
        return rcopy(ref, ref, ssem.at[kind], rsem.at[kind], x * NZ + mod(z + by + NZ, NZ), tok)

    for kind in range(2):
        for by in (2, -2, 1, -1):
            z_copy(kind, 0, by, z_s, z_r).start()

    loads[4].wait()
    expand = (iota((NB, ROWS), 0) == iota((NB, ROWS), 1) >> 4).astype(BF)
    wide = matmul(sm_ref[...].reshape(ROWS, NB), expand)
    same = (iota((ROWS, ROWS), 1) & 15) == (iota((ROWS, ROWS), 0) >> 5)
    spread[...] = jnp.where(same, wide, 0.0).astype(BF)

    wait_recv(lens_rx.at[pl.ds(0, PAGES - 1)], lens_r)
    lens = lens_rx[:, 0, :]
    lens = jnp.concatenate([lens] * 4, axis=1)
    kept = jnp.clip(lens - tok * ROWS, 0, ROWS)
    who = iota((PAGES, ROWS), 0)
    lane_page = iota((PAGES, ROWS), 1) >> 4
    shift = jnp.sum(jnp.where(who < page, kept, 0), axis=0, keepdims=True)
    start_of = jnp.sum(jnp.where(who < lane_page, kept, 0), axis=0, keepdims=True)
    stop_of = start_of + jnp.sum(jnp.where(who == lane_page, kept, 0), axis=0, keepdims=True)

    @pl.loop(0, 4)
    def _(r):
        rows = pl.ds(pl.multiple_of(r * 128, 128), 128)
        slot = iota((128, ROWS), 0) + r * 128
        turn = (((iota((128, ROWS), 1) + shift) & (ROWS - 1)) == slot).astype(BF)
        pre[rows, :] = matmul(turn, xm[...]).astype(BF)
        psel[rows, :] = matmul(turn, spread[...]).astype(BF)

    los, his = [gu_lo, wd_lo], [gu_hi, wd_hi]
    mid = (NZ - SPLIT + 1) // 2

    def xlo(xx, cut, kind):
        zs = [pl.ds(0, SPLIT), pl.ds(0, SPLIT // 2), pl.ds(SPLIT // 2, SPLIT - SPLIT // 2)][cut]
        return los[kind].at[c, yh, yl, xx, zs]

    def yhi(yy, cut, kind):
        zs = [pl.ds(0, NZ - SPLIT), pl.ds(0, mid), pl.ds(mid, NZ - SPLIT - mid)][cut]
        return his[kind].at[c, x, div(yy, 2), mod(yy, 2), zs]

    def ylo(yy, cut, kind):
        xs = [pl.ds(0, 4), pl.ds(0, 2), pl.ds(2, 2)][cut]
        return los[kind].at[c, div(yy, 2), mod(yy, 2), xs]

    def xhi(xx, cut, kind):
        ys = [pl.ds(0, 2), pl.ds(0, 1), pl.ds(1, 1)][cut]
        return his[kind].at[c, xx, ys]

    def xdev(by):
        return mod(x + by, NX) * NZ + z, tok

    def ydev(by):
        return page, mod(y + by, NY) * NC + c

    rings = [[(xlo, x, xdev), (yhi, y, ydev)], [(ylo, y, ydev), (xhi, x, xdev)]]

    def ring_copy(stage, kind, hop, which, way):
        piece, me, dev = rings[stage][which]
        by = 1 if way == 0 else 3
        ref = piece(me, 0, kind) if hop == 0 else piece(mod(me + 4 - by, 4), 1 + way, kind)
        src = ref
        if stage == 0 and hop == 0:
            src = zunits[kind].at[pl.ds(0, SPLIT) if which == 0 else pl.ds(SPLIT, NZ - SPLIT)]
        i = stage * 16 + kind * 8 + hop * 4 + which * 2 + way
        return rcopy(src, ref, ring_s.at[i], ring_r.at[i], *dev(by))

    def arriving(stage, kind, hop, which, way):
        piece, me, dev = rings[stage][which]
        by = 1 if way == 0 else 3
        return piece(mod(me + 4 - by, 4), 0, kind) if hop == 0 else piece(mod(me + 2, 4), 1 + way, kind)

    def ring_arrived(stage, kind, hop, which, way):
        i = stage * 16 + kind * 8 + hop * 4 + which * 2 + way
        wait_recv(arriving(stage, kind, hop, which, way), ring_r.at[i])

    both = [(which, way) for which in range(2) for way in range(2)]

    def core_copy(i, ref):
        copy = rcopy(ref, ref, core_s.at[i], core_r.at[i], page, sibling)
        copy.start()
        return copy

    def turn_rows(h):
        at, n = CHUNKS[h]
        own[h].wait()
        wait_recv(frecv[h].at[pl.ds(0, TOKS - 1)], tok_r.at[h])

        @pl.loop(0, 4)
        def _(r):
            rows = pl.ds(pl.multiple_of(r * 128, 128), 128)
            second = matmul(psel[rows, :], frecv[h][...].reshape(ROWS, n))
            mixed = (pre[rows, at : at + n].astype(F32) + second).astype(BF)
            p1tx[h][pl.ds(r * 8, 8)] = mixed.reshape(8, PER, n)

        @pl.loop(1, PAGES)
        def _(k):
            to = mod(page + k, PAGES)
            rcopy(p1tx[h].at[to], p1rx[h].at[page], p1_s.at[h], p1_r.at[h], to, tok).start()

        own1.append(pltpu.make_async_copy(p1tx[h].at[page], p1rx[h].at[page], own_s.at[3 + h]))
        own1[h].start()

    def pack_rows(h):
        n = CHUNKS[h][1]
        own1[h].wait()
        wait_recv(p1rx[h].at[pl.ds(0, PAGES - 1)], p1_r.at[h])

        @pl.loop(0, 4)
        def _(r):
            rows = pl.ds(pl.multiple_of(r * 128, 128), 128)
            mixed = matmul(picks[rows, :], p1rx[h][...].reshape(ROWS, n))
            p2tx[h][pl.ds(r * 8, 8)] = mixed.astype(BF).reshape(8, PER, n)

        @pl.loop(1, PAGES)
        def _(k):
            to = mod(page + k, PAGES)
            rcopy(p2tx[h].at[to], p2rx[h].at[page], p2_s.at[h], p2_r.at[h], to, tok).start()

        own2.append(pltpu.make_async_copy(p2tx[h].at[page], p2rx[h].at[page], own_s.at[6 + h]))
        own2[h].start()

    own1, own2, keeps, cores = [], [], [], [[], []]
    for kind in range(2):
        wait_recv(zunits[kind].at[pl.ds(0, 4)], z_r.at[kind])
        z_copy(kind, -2, 1, z2_s, z2_r).start()
        z_copy(kind, 2, -1, z2_s, z2_r).start()
        z_copy(kind, 4 * kind - 2, 2 - 4 * kind, z2_s, z2_r).start()
    turn_rows(0)
    for kind in range(2):
        wait_recv(zunits[kind].at[pl.ds(0, 3)], z2_r.at[kind])
        for which, way in both:
            ring_copy(0, kind, 0, which, way).start()
        for which in range(2):
            piece, me, dev = rings[0][which]
            span = pl.ds(0, SPLIT) if which == 0 else pl.ds(SPLIT, NZ - SPLIT)
            copy = pltpu.make_async_copy(zunits[kind].at[span], piece(me, 0, kind), keep_s.at[kind * 2 + which])
            copy.start()
            keeps.append(copy)
    turn_rows(1)
    for kind in range(2):
        for which, way in both:
            ring_arrived(0, kind, 0, which, way)
            ring_copy(0, kind, 1, which, way).start()
    for copy in keeps:
        copy.wait()
    turn_rows(2)

    @pl.loop(0, 4)
    def _(r):
        row = iota((128, ROWS), 0) + r * 128
        col = iota((128, ROWS), 1)
        target = (row >> 4) * ROWS + page * PER + (row & 15)
        pick = ((row & 15) == (col & 15)) & (target >= start_of) & (target < stop_of)
        picks[pl.ds(pl.multiple_of(r * 128, 128), 128), :] = pick.astype(BF)

    for kind in range(2):
        for which, way in both:
            ring_arrived(0, kind, 1, which, way)
        for which, way in both:
            ring_copy(1, kind, 0, which, way).start()
    pack_rows(0)
    for kind in range(2):
        for which in range(2):
            piece, me, dev = rings[1][which]
            cores[kind].append(core_copy(kind * 10 + which, piece(me, 0, kind)))
    pack_rows(1)
    for kind in range(2):
        for which, way in both:
            ring_arrived(1, kind, 0, which, way)
            ring_copy(1, kind, 1, which, way).start()
            cores[kind].append(core_copy(kind * 10 + 2 + which * 2 + way, arriving(1, kind, 0, which, way)))
        if kind == 0:
            pack_rows(2)

    def last_hop(kind):
        for which, way in both:
            ring_arrived(1, kind, 1, which, way)
            cores[kind].append(core_copy(kind * 10 + 6 + which * 2 + way, arriving(1, kind, 1, which, way)))

    last_hop(0)

    for h in range(len(CHUNKS)):
        own2[h].wait()
        wait_recv(p2rx[h].at[pl.ds(0, PAGES - 1)], p2_r.at[h])

    @pl.loop(0, 4)
    def _(r):
        rows = pl.ds(pl.multiple_of(r * 128, 128), 128)
        mixed = [p2rx[h][pl.ds(r * 8, 8)].reshape(128, n).astype(F32) for h, (at, n) in enumerate(CHUNKS)]
        total = sum(jnp.sum(v * v, axis=-1, keepdims=True) for v in mixed)
        scale = lax.rsqrt(total / D + EPS)
        for v, (at, n) in zip(mixed, CHUNKS):
            ynorm[rows, at : at + n] = (v * scale).astype(BF)

    for copy in cores[0]:
        copy.wait_recv()

    def unit(kind, core, xx, zz, ys):
        if zz < SPLIT:
            return los[kind][core, :, ys, xx, zz]
        return his[kind][core, xx, :, ys, zz - SPLIT]

    @pl.loop(0, 4)
    def _(xx):
        for t in range(2):
            zs = range(4 * t, 4 * t + 4)
            rows = [
                jnp.concatenate([unit(0, core, xx, zz, slice(None)).reshape(64, D) for zz in zs], axis=0)
                for core in range(2)
            ]
            gate, up = matmul_nt(ynorm[...], rows[0]), matmul_nt(ynorm[...], rows[1])
            cols = pl.ds(pl.multiple_of(xx * 512 + t * 256, 256), 256)
            hid[:, cols] = (gate / (1.0 + jnp.exp(-gate)) * up).astype(BF)

    last_hop(1)
    for copy in cores[1]:
        copy.wait_recv()

    for t, h in enumerate((0, 1, 2, 2)):
        at = t * 256 - CHUNKS[h][0]
        total = p2rx[h][:, :, at : at + 256].reshape(ROWS, 256).astype(F32)
        for q in range(4):
            down = jnp.concatenate([unit(1, q % 2, t, zz, q // 2).reshape(32, 512) for zz in range(NZ)], axis=0)
            total = total + matmul_nt(hid[:, q * 512 : (q + 1) * 512], down)
        o_ref[:, t * 256 : (t + 1) * 256] = total.astype(BF)

    wait_send(gu_rx, gu_s)
    wait_send(wd_rx, wd_s)
    wait_send(lens_rx.at[pl.ds(0, PAGES - 1)], lens_s)
    for kind in range(2):
        wait_send(zunits[kind].at[pl.ds(0, 4)], z_s.at[kind])
        wait_send(zunits[kind].at[pl.ds(0, 3)], z2_s.at[kind])
    for h in range(len(CHUNKS)):
        wait_send(frecv[h].at[pl.ds(0, TOKS - 1)], tok_s.at[h])
        wait_send(p1tx[h].at[pl.ds(0, PAGES - 1)], p1_s.at[h])
        wait_send(p2tx[h].at[pl.ds(0, PAGES - 1)], p2_s.at[h])
    for stage in range(2):
        for kind in range(2):
            for hop in range(2):
                for which, way in both:
                    ring_copy(stage, kind, hop, which, way).wait_send()
    for copy in cores[0] + cores[1]:
        copy.wait_send()


def per_device(tile_tokens, page_lengths, occupancy, block_mix, stride_mix, w_gate_up, w_down):
    vmem = pl.BlockSpec(memory_space=pltpu.VMEM)
    smem = pl.BlockSpec(memory_space=pltpu.SMEM)
    dma = pltpu.SemaphoreType.DMA
    anywhere = pl.BlockSpec(memory_space=pltpu.HBM)
    packed = pl.pallas_call(
        body,
        out_shape=jax.ShapeDtypeStruct((ROWS, D), BF),
        in_specs=[smem, smem] + [anywhere] * 5,
        out_specs=vmem,
        scratch_shapes=[
            pltpu.VMEM((ROWS, D), BF),
            pltpu.VMEM((4, BLK, BLK), BF),
            pltpu.VMEM((PER, NB, NB), BF),
            pltpu.VMEM((2, 8, D), BF),
            pltpu.VMEM((4, FF), BF),
            pltpu.VMEM((PAGES, 1, 128), jnp.int32),
            pltpu.VMEM((2, 16, D), BF),
            pltpu.VMEM((16, D), BF),
            pltpu.VMEM((4, 16, 512), BF),
            pltpu.VMEM((3, 16, 512), BF),
            pltpu.VMEM((NZ, 16, D), BF),
            pltpu.VMEM((NZ, 16, 512), BF),
            pltpu.VMEM((NC, 2, 2, NX, SPLIT, 16, D), BF),
            pltpu.VMEM((NC, NX, 2, 2, NZ - SPLIT, 16, D), BF),
            pltpu.VMEM((NC, 2, 2, NX, SPLIT, 16, 512), BF),
            pltpu.VMEM((NC, NX, 2, 2, NZ - SPLIT, 16, 512), BF),
            pltpu.VMEM((ROWS, D), BF),
            pltpu.VMEM((ROWS, ROWS), BF),
            pltpu.VMEM((ROWS, D), BF),
            pltpu.VMEM((ROWS, ROWS), BF),
            pltpu.VMEM((ROWS, ROWS), BF),
            pltpu.VMEM((ROWS, D), BF),
            pltpu.VMEM((ROWS, FF), BF),
            *[[pltpu.VMEM((TOKS, 4, PER, n), BF) for at, n in CHUNKS] for k in range(2)],
            *[[pltpu.VMEM((PAGES, PER, n), BF) for at, n in CHUNKS] for k in range(4)],
        ]
        + [dma] * 6
        + [dma((2,))] * 2
        + [dma((3,))] * 6
        + [dma((32,)), dma((32,)), dma((20,)), dma((20,)), dma((9,)), dma((5,)), dma((4,)), dma((2,)), dma((2,))],
        compiler_params=pltpu.CompilerParams(
            collective_id=0, has_side_effects=True, vmem_limit_bytes=48 * 1024 * 1024
        ),
    )(
        page_lengths, occupancy,
        *(
            pltpu.with_memory_space_constraint(v, pltpu.HBM)
            for v in (tile_tokens[0], block_mix, stride_mix, jnp.swapaxes(w_gate_up, 1, 2), w_down.T)
        ),
    )
    return packed.reshape(1, ROWS, D)


def solution(mesh):
    return jax.shard_map(
        per_device,
        mesh=mesh,
        in_specs=(
            P("page", "tok", None),
            P("page"),
            P("page", "tok"),
            P("tok", None, None),
            P("tok", None, None),
            P(None, None, ("page", "tok")),
            P(None, ("page", "tok")),
        ),
        out_specs=P("tok", "page", None),
        check_vma=False,
    )
```

```python
import jax
import jax.numpy as jnp
from jax import lax
from jax.experimental import pallas as pl
from jax.experimental.pallas import tpu as pltpu
from jax.sharding import PartitionSpec as P

NX, NZ, NY, NC = 4, 8, 4, 2
PAGES, TOKS = 32, 8
ROWS, D, FF = 512, 1024, 2048
BLK, NB, PER = 128, 32, 16
EPS = 1e-05
SPLITS = (5, 6)
CHUNKS = ((0, 256), (256, 256), (512, 512))
MESH = pl.DeviceIdType.MESH
NT = (((1,), (1,)), ((), ()))
BF, F32 = jnp.bfloat16, jnp.float32


def mod(a, n):
    return lax.rem(a, jnp.int32(n))


def div(a, n):
    return lax.div(a, jnp.int32(n))


def iota(shape, dim):
    return lax.broadcasted_iota(jnp.int32, shape, dim)


def matmul(a, b):
    return jnp.dot(a, b, preferred_element_type=F32)


def matmul_nt(a, b):
    return lax.dot_general(a, b, NT, preferred_element_type=F32)


def rms_round(values):
    scale = lax.rsqrt(jnp.mean(values * values, axis=-1, keepdims=True) + EPS)
    return (values * scale).astype(BF)


def body(
    len_ref, occ_ref, x_hbm, bm_hbm, sm_hbm, wg_hbm, wd_hbm, o_ref,
    x_ref, bm_ref, sm_ref, wg_ref, wd_ref,
    lens_rx, gu_tx, gu_rx, wd_tx, wd_rx, zunit_gu, zunit_wd, gu_lo, gu_hi, wd_lo, wd_hi, xm, spread, pre, psel, picks,
    sums, scales, hid,
    fsend, frecv, p1tx, p1rx, p2tx, p2rx,
    lens_s, lens_r, gu_s, gu_r, wd_s, wd_r, z_s, z_r, tok_s, tok_r,
    p1_s, p1_r, p2_s, p2_r, ring_s, ring_r, core_s, core_r, own_s, in_s, keep_s, z2_s, z2_r,
):
    page, tok = lax.axis_index("page"), lax.axis_index("tok")
    x, z = div(page, NZ), mod(page, NZ)
    y, c = div(tok, NC), mod(tok, NC)
    yh, yl = div(y, 2), mod(y, 2)
    sibling = tok + 1 - 2 * c

    def rcopy(src, dst, ssem, rsem, to_page, to_tok):
        return pltpu.make_async_remote_copy(
            src_ref=src, dst_ref=dst, send_sem=ssem, recv_sem=rsem,
            device_id=(to_page, to_tok), device_id_type=MESH,
        )

    def wait_recv(ref, sem):
        rcopy(ref, ref, sem, sem, page, sibling).wait_recv()

    def wait_send(ref, sem):
        rcopy(ref, ref, sem, sem, page, sibling).wait_send()

    loads = [
        pltpu.make_async_copy(src, dst, in_s.at[i])
        for i, (src, dst) in enumerate(
            [(wg_hbm, wg_ref), (wd_hbm, wd_ref), (x_hbm, x_ref), (bm_hbm, bm_ref), (sm_hbm, sm_ref)]
        )
    ]
    for load in loads:
        load.start()
    barrier = pltpu.get_barrier_semaphore()

    @pl.loop(1, PAGES)
    def _(k):
        pl.semaphore_signal(barrier, inc=1, device_id=(mod(page + k, PAGES), tok), device_id_type=MESH)

    @pl.loop(1, TOKS)
    def _(k):
        pl.semaphore_signal(barrier, inc=1, device_id=(page, mod(tok + k, TOKS)), device_id_type=MESH)

    length = len_ref[0]
    loads[0].wait()
    loads[1].wait()
    place8 = (iota((16, 8), 0) == iota((16, 8), 1) + 8 * c).astype(BF)
    place4 = (iota((16, 4), 0) == iota((16, 4), 1) + 4 * mod(tok, 4)).astype(BF)
    for g in range(2):
        gu_tx[g] = matmul(place8, wg_ref[g]).astype(BF)
    wd_all = matmul(place4, wd_ref[...]).astype(BF)
    for q in range(4):
        wd_tx[q] = wd_all[:, q * 512 : (q + 1) * 512]
    lens_rx[page] = jnp.full((1, 128), length, jnp.int32)

    loads[2].wait()
    loads[3].wait()
    for b in range(4):
        limit = length * occ_ref[0, b] - tok * ROWS - b * BLK
        rows = slice(b * BLK, (b + 1) * BLK)
        live = iota((BLK, D), 0) < limit
        masked = jnp.where(live, x_ref[rows, :].astype(F32), 0.0)
        xm[rows, :] = masked.astype(BF)
        first = matmul(bm_ref[b], rms_round(masked)).astype(BF)
        for h, (at, n) in enumerate(CHUNKS):
            fsend[h][:, b] = first[:, at : at + n].reshape(TOKS, PER, n)

    pl.semaphore_wait(barrier, PAGES - 1 + TOKS - 1)

    rcopy(gu_tx.at[1 - c], gu_rx, gu_s, gu_r, page, sibling).start()
    half = 4 * div(tok, 4)
    for k in range(1, 4):
        q = mod(tok + k, 4)
        rcopy(wd_tx.at[q], wd_rx.at[3 - k], wd_s, wd_r, page, half + q).start()

    own = []

    def send_first(h):
        own.append(pltpu.make_async_copy(fsend[h].at[tok], frecv[h].at[tok], own_s.at[h]))
        own[h].start()

        @pl.loop(1, TOKS)
        def _(k):
            to = mod(tok + k, TOKS)
            rcopy(fsend[h].at[to], frecv[h].at[tok], tok_s.at[h], tok_r.at[h], page, to).start()

    send_first(0)

    @pl.loop(1, PAGES)
    def _(k):
        rcopy(lens_rx.at[page], lens_rx.at[page], lens_s, lens_r, mod(page + k, PAGES), tok).start()

    wait_recv(gu_rx, gu_r)
    wait_recv(wd_rx, wd_r)
    zunit_gu[z] = gu_tx[c] + gu_rx[...]
    zunit_wd[z] = wd_tx[mod(tok, 4)] + wd_rx[0] + wd_rx[1] + wd_rx[2]
    zunits = [zunit_gu, zunit_wd]

    def z_copy(kind, origin, by, ssem, rsem):
        ref = zunits[kind].at[mod(z + origin + NZ, NZ)]
        return rcopy(ref, ref, ssem.at[kind], rsem.at[kind], x * NZ + mod(z + by + NZ, NZ), tok)

    for kind in range(2):
        for by in (2, -2, 1, -1):
            z_copy(kind, 0, by, z_s, z_r).start()
    send_first(1)
    send_first(2)

    loads[4].wait()
    expand = (iota((NB, ROWS), 0) == iota((NB, ROWS), 1) >> 4).astype(BF)
    wide = matmul(sm_ref[...].reshape(ROWS, NB), expand)
    same = (iota((ROWS, ROWS), 1) & 15) == (iota((ROWS, ROWS), 0) >> 5)
    spread[...] = jnp.where(same, wide, 0.0).astype(BF)

    wait_recv(lens_rx.at[pl.ds(0, PAGES - 1)], lens_r)
    lens = lens_rx[:, 0, :]
    lens = jnp.concatenate([lens] * 4, axis=1)
    kept = jnp.clip(lens - tok * ROWS, 0, ROWS)
    who = iota((PAGES, ROWS), 0)
    lane_page = iota((PAGES, ROWS), 1) >> 4
    shift = jnp.sum(jnp.where(who < page, kept, 0), axis=0, keepdims=True)
    start_of = jnp.sum(jnp.where(who < lane_page, kept, 0), axis=0, keepdims=True)
    stop_of = start_of + jnp.sum(jnp.where(who == lane_page, kept, 0), axis=0, keepdims=True)

    @pl.loop(0, 4)
    def _(r):
        rows = pl.ds(pl.multiple_of(r * 128, 128), 128)
        slot = iota((128, ROWS), 0) + r * 128
        turn = (((iota((128, ROWS), 1) + shift) & (ROWS - 1)) == slot).astype(BF)
        pre[rows, :] = matmul(turn, xm[...]).astype(BF)
        psel[rows, :] = matmul(turn, spread[...]).astype(BF)

    los, his = [gu_lo, wd_lo], [gu_hi, wd_hi]

    def xlo(xx, cut, kind):
        n = SPLITS[kind]
        zs = [pl.ds(0, n), pl.ds(0, n // 2), pl.ds(n // 2, n - n // 2)][cut]
        return los[kind].at[c, yh, yl, xx, zs]

    def yhi(yy, cut, kind):
        n = NZ - SPLITS[kind]
        mid = (n + 1) // 2
        zs = [pl.ds(0, n), pl.ds(0, mid), pl.ds(mid, n - mid)][cut]
        return his[kind].at[c, x, div(yy, 2), mod(yy, 2), zs]

    def ylo(yy, cut, kind):
        xs = [pl.ds(0, 4), pl.ds(0, 2), pl.ds(2, 2)][cut]
        return los[kind].at[c, div(yy, 2), mod(yy, 2), xs]

    def xhi(xx, cut, kind):
        ys = [pl.ds(0, 2), pl.ds(0, 1), pl.ds(1, 1)][cut]
        return his[kind].at[c, xx, ys]

    def xdev(by):
        return mod(x + by, NX) * NZ + z, tok

    def ydev(by):
        return page, mod(y + by, NY) * NC + c

    rings = [[(xlo, x, xdev), (yhi, y, ydev)], [(ylo, y, ydev), (xhi, x, xdev)]]

    def ring_copy(stage, kind, hop, which, way):
        piece, me, dev = rings[stage][which]
        by = 1 if way == 0 else 3
        ref = piece(me, 0, kind) if hop == 0 else piece(mod(me + 4 - by, 4), 1 + way, kind)
        src = ref
        if stage == 0 and hop == 0:
            src = zunits[kind].at[pl.ds(0, SPLITS[kind]) if which == 0 else pl.ds(SPLITS[kind], NZ - SPLITS[kind])]
        i = stage * 16 + kind * 8 + hop * 4 + which * 2 + way
        return rcopy(src, ref, ring_s.at[i], ring_r.at[i], *dev(by))

    def arriving(stage, kind, hop, which, way):
        piece, me, dev = rings[stage][which]
        by = 1 if way == 0 else 3
        return piece(mod(me + 4 - by, 4), 0, kind) if hop == 0 else piece(mod(me + 2, 4), 1 + way, kind)

    def ring_arrived(stage, kind, hop, which, way):
        i = stage * 16 + kind * 8 + hop * 4 + which * 2 + way
        wait_recv(arriving(stage, kind, hop, which, way), ring_r.at[i])

    def pass_on(kind, which, by, src=None):
        j = mod((x, y)[which] + by, 4)
        ref = (los[kind].at[c, yh, yl, j], his[kind].at[c, x, div(j, 2), mod(j, 2)])[which]
        for way in range(2):
            i = 16 + kind * 8 + which * 2 + way
            dev = (ydev, xdev)[which](1 if way == 0 else 3)
            rcopy(ref if src is None else src, ref, ring_s.at[i], ring_r.at[i], *dev).start()

    both = [(which, way) for which in range(2) for way in range(2)]

    def core_copy(i, ref):
        copy = rcopy(ref, ref, core_s.at[i], core_r.at[i], page, sibling)
        copy.start()
        return copy

    def turn_rows(h):
        at, n = CHUNKS[h]
        own[h].wait()
        wait_recv(frecv[h].at[pl.ds(0, TOKS - 1)], tok_r.at[h])

        @pl.loop(0, 4)
        def _(r):
            rows = pl.ds(pl.multiple_of(r * 128, 128), 128)
            second = matmul(psel[rows, :], frecv[h][...].reshape(ROWS, n))
            mixed = (pre[rows, at : at + n].astype(F32) + second).astype(BF)
            p1tx[h][pl.ds(r * 8, 8)] = mixed.reshape(8, PER, n)

        @pl.loop(1, PAGES)
        def _(k):
            to = mod(page + k, PAGES)
            rcopy(p1tx[h].at[to], p1rx[h].at[page], p1_s.at[h], p1_r.at[h], to, tok).start()

        own1.append(pltpu.make_async_copy(p1tx[h].at[page], p1rx[h].at[page], own_s.at[3 + h]))
        own1[h].start()

    def pack_rows(h):
        n = CHUNKS[h][1]
        own1[h].wait()
        wait_recv(p1rx[h].at[pl.ds(0, PAGES - 1)], p1_r.at[h])

        @pl.loop(0, 4)
        def _(r):
            rows = pl.ds(pl.multiple_of(r * 128, 128), 128)
            mixed = matmul(picks[rows, :], p1rx[h][...].reshape(ROWS, n))
            p2tx[h][pl.ds(r * 8, 8)] = mixed.astype(BF).reshape(8, PER, n)

        @pl.loop(1, PAGES)
        def _(k):
            to = mod(page + k, PAGES)
            rcopy(p2tx[h].at[to], p2rx[h].at[page], p2_s.at[h], p2_r.at[h], to, tok).start()

        own2.append(pltpu.make_async_copy(p2tx[h].at[page], p2rx[h].at[page], own_s.at[6 + h]))
        own2[h].start()

    own1, own2, keeps, cores = [], [], [], [[], []]
    for kind in range(2):
        wait_recv(zunits[kind].at[pl.ds(0, 4)], z_r.at[kind])
        z_copy(kind, -2, 1, z2_s, z2_r).start()
        z_copy(kind, 2, -1, z2_s, z2_r).start()
        z_copy(kind, 4 * kind - 2, 2 - 4 * kind, z2_s, z2_r).start()
    turn_rows(0)
    for kind in range(2):
        wait_recv(zunits[kind].at[pl.ds(0, 3)], z2_r.at[kind])
        for which, way in both:
            ring_copy(0, kind, 0, which, way).start()
        for which in range(2):
            piece, me, dev = rings[0][which]
            span = pl.ds(0, SPLITS[kind]) if which == 0 else pl.ds(SPLITS[kind], NZ - SPLITS[kind])
            copy = pltpu.make_async_copy(zunits[kind].at[span], piece(me, 0, kind), keep_s.at[kind * 2 + which])
            copy.start()
            pass_on(kind, which, 0, zunits[kind].at[span])
            keeps.append(copy)
    turn_rows(1)
    for kind in range(2):
        for which, way in both:
            ring_arrived(0, kind, 0, which, way)
            ring_copy(0, kind, 1, which, way).start()
        for which, way in both:
            pass_on(kind, which, 3 if way == 0 else 1)
    for copy in keeps:
        copy.wait()
    turn_rows(2)

    @pl.loop(0, 4)
    def _(r):
        row = iota((128, ROWS), 0) + r * 128
        col = iota((128, ROWS), 1)
        target = (row >> 4) * ROWS + page * PER + (row & 15)
        pick = ((row & 15) == (col & 15)) & (target >= start_of) & (target < stop_of)
        picks[pl.ds(pl.multiple_of(r * 128, 128), 128), :] = pick.astype(BF)

    for kind in range(2):
        for which, way in both:
            ring_arrived(0, kind, 1, which, way)
        for which in range(2):
            pass_on(kind, which, 2)
    pack_rows(0)
    for kind in range(2):
        for which in range(2):
            piece, me, dev = rings[1][which]
            cores[kind].append(core_copy(kind * 10 + which, piece(me, 0, kind)))
    pack_rows(1)
    for kind in range(2):
        for which, way in both:
            ring_arrived(1, kind, 0, which, way)
            ring_copy(1, kind, 1, which, way).start()
            cores[kind].append(core_copy(kind * 10 + 2 + which * 2 + way, arriving(1, kind, 0, which, way)))
        if kind == 0:
            pack_rows(2)

    def last_hop(kind):
        for which, way in both:
            ring_arrived(1, kind, 1, which, way)
            cores[kind].append(core_copy(kind * 10 + 6 + which * 2 + way, arriving(1, kind, 1, which, way)))

    last_hop(0)

    def packed_chunk(h):
        return p2rx[h][...].reshape(ROWS, CHUNKS[h][1])

    def squares(h):
        wide = packed_chunk(h).astype(F32)
        return jnp.sum(wide * wide, axis=-1, keepdims=True)

    def unit(kind, core, xx, zz, ys, cols):
        if zz < SPLITS[kind]:
            return los[kind][core, :, ys, xx, zz, :, cols]
        return his[kind][core, xx, :, ys, zz - SPLITS[kind], :, cols]

    def gate_rows(core, xx, t, cols, n):
        parts = [unit(0, core, xx, zz, slice(None), cols).reshape(64, n) for zz in range(4 * t, 4 * t + 4)]
        return jnp.concatenate(parts, axis=0)

    def arrived_chunk(h):
        own2[h].wait()
        wait_recv(p2rx[h].at[pl.ds(0, PAGES - 1)], p2_r.at[h])

    for copy in cores[0]:
        copy.wait_recv()
    arrived_chunk(0)
    arrived_chunk(1)

    @pl.loop(0, 4)
    def _(xx):
        for t in range(2):
            cols = pl.ds(pl.multiple_of(xx * 512 + t * 256, 256), 256)
            for core in range(2):
                sums[core, :, cols] = sum(
                    matmul_nt(packed_chunk(h), gate_rows(core, xx, t, slice(h * 256, h * 256 + 256), 256)) for h in range(2)
                )

    first_squares = squares(0) + squares(1)
    last_hop(1)
    arrived_chunk(2)
    scale = lax.rsqrt((first_squares + squares(2)) / D + EPS)
    scales[...] = jnp.broadcast_to(scale, (ROWS, 256))

    @pl.loop(0, 4)
    def _(xx):
        for t in range(2):
            cols = pl.ds(pl.multiple_of(xx * 512 + t * 256, 256), 256)
            gate, up = [
                (sums[core, :, cols] + matmul_nt(packed_chunk(2), gate_rows(core, xx, t, slice(512, D), 512))) * scales[...]
                for core in range(2)
            ]
            hid[:, cols] = (gate / (1.0 + jnp.exp(-gate)) * up).astype(BF)

    for copy in cores[1]:
        copy.wait_recv()

    for t, h in enumerate((0, 1, 2, 2)):
        at = t * 256 - CHUNKS[h][0]
        total = p2rx[h][:, :, at : at + 256].reshape(ROWS, 256).astype(F32)
        for q in range(4):
            down = jnp.concatenate([unit(1, q % 2, t, zz, q // 2, slice(None)).reshape(32, 512) for zz in range(NZ)], axis=0)
            total = total + matmul_nt(hid[:, q * 512 : (q + 1) * 512], down)
        o_ref[:, t * 256 : (t + 1) * 256] = total.astype(BF)

    wait_send(gu_rx, gu_s)
    wait_send(wd_rx, wd_s)
    wait_send(lens_rx.at[pl.ds(0, PAGES - 1)], lens_s)
    for kind in range(2):
        wait_send(zunits[kind].at[pl.ds(0, 4)], z_s.at[kind])
        wait_send(zunits[kind].at[pl.ds(0, 3)], z2_s.at[kind])
    for h in range(len(CHUNKS)):
        wait_send(frecv[h].at[pl.ds(0, TOKS - 1)], tok_s.at[h])
        wait_send(p1tx[h].at[pl.ds(0, PAGES - 1)], p1_s.at[h])
        wait_send(p2tx[h].at[pl.ds(0, PAGES - 1)], p2_s.at[h])
    for stage in range(2):
        for kind in range(2):
            for hop in range(2):
                for which, way in both:
                    ring_copy(stage, kind, hop, which, way).wait_send()
    for copy in cores[0] + cores[1]:
        copy.wait_send()


def per_device(tile_tokens, page_lengths, occupancy, block_mix, stride_mix, w_gate_up, w_down):
    vmem = pl.BlockSpec(memory_space=pltpu.VMEM)
    smem = pl.BlockSpec(memory_space=pltpu.SMEM)
    dma = pltpu.SemaphoreType.DMA
    anywhere = pl.BlockSpec(memory_space=pltpu.HBM)
    packed = pl.pallas_call(
        body,
        out_shape=jax.ShapeDtypeStruct((ROWS, D), BF),
        in_specs=[smem, smem] + [anywhere] * 5,
        out_specs=vmem,
        scratch_shapes=[
            pltpu.VMEM((ROWS, D), BF),
            pltpu.VMEM((4, BLK, BLK), BF),
            pltpu.VMEM((PER, NB, NB), BF),
            pltpu.VMEM((2, 8, D), BF),
            pltpu.VMEM((4, FF), BF),
            pltpu.VMEM((PAGES, 1, 128), jnp.int32),
            pltpu.VMEM((2, 16, D), BF),
            pltpu.VMEM((16, D), BF),
            pltpu.VMEM((4, 16, 512), BF),
            pltpu.VMEM((3, 16, 512), BF),
            pltpu.VMEM((NZ, 16, D), BF),
            pltpu.VMEM((NZ, 16, 512), BF),
            pltpu.VMEM((NC, 2, 2, NX, SPLITS[0], 16, D), BF),
            pltpu.VMEM((NC, NX, 2, 2, NZ - SPLITS[0], 16, D), BF),
            pltpu.VMEM((NC, 2, 2, NX, SPLITS[1], 16, 512), BF),
            pltpu.VMEM((NC, NX, 2, 2, NZ - SPLITS[1], 16, 512), BF),
            pltpu.VMEM((ROWS, D), BF),
            pltpu.VMEM((ROWS, ROWS), BF),
            pltpu.VMEM((ROWS, D), BF),
            pltpu.VMEM((ROWS, ROWS), BF),
            pltpu.VMEM((ROWS, ROWS), BF),
            pltpu.VMEM((2, ROWS, FF), F32),
            pltpu.VMEM((ROWS, 256), F32),
            pltpu.VMEM((ROWS, FF), BF),
            *[[pltpu.VMEM((TOKS, 4, PER, n), BF) for at, n in CHUNKS] for k in range(2)],
            *[[pltpu.VMEM((PAGES, PER, n), BF) for at, n in CHUNKS] for k in range(4)],
        ]
        + [dma] * 6
        + [dma((2,))] * 2
        + [dma((3,))] * 6
        + [dma((32,)), dma((32,)), dma((20,)), dma((20,)), dma((9,)), dma((5,)), dma((4,)), dma((2,)), dma((2,))],
        compiler_params=pltpu.CompilerParams(
            collective_id=0, has_side_effects=True, vmem_limit_bytes=48 * 1024 * 1024
        ),
    )(
        page_lengths, occupancy,
        *(
            pltpu.with_memory_space_constraint(v, pltpu.HBM)
            for v in (tile_tokens[0], block_mix, stride_mix, jnp.swapaxes(w_gate_up, 1, 2), w_down.T)
        ),
    )
    return packed.reshape(1, ROWS, D)


def solution(mesh):
    return jax.shard_map(
        per_device,
        mesh=mesh,
        in_specs=(
            P("page", "tok", None),
            P("page"),
            P("page", "tok"),
            P("tok", None, None),
            P("tok", None, None),
            P(None, None, ("page", "tok")),
            P(None, ("page", "tok")),
        ),
        out_specs=P("tok", "page", None),
        check_vma=False,
    )
```

```python
import jax
import jax.numpy as jnp
from jax import lax
from jax.experimental import pallas as pl
from jax.experimental.pallas import tpu as pltpu
from jax.sharding import PartitionSpec as P

NX, NZ, NY, NC = 4, 8, 4, 2
PAGES, TOKS = 32, 8
ROWS, D, FF = 512, 1024, 2048
BLK, NB, PER = 128, 32, 16
EPS = 1e-05
SPLITS = (6, 5)
CHUNKS = ((0, 256), (256, 256), (512, 512))
MESH = pl.DeviceIdType.MESH
NT = (((1,), (1,)), ((), ()))
BF, F32 = jnp.bfloat16, jnp.float32


def mod(a, n):
    return lax.rem(a, jnp.int32(n))


def div(a, n):
    return lax.div(a, jnp.int32(n))


def iota(shape, dim):
    return lax.broadcasted_iota(jnp.int32, shape, dim)


def matmul(a, b):
    return jnp.dot(a, b, preferred_element_type=F32)


def matmul_nt(a, b):
    return lax.dot_general(a, b, NT, preferred_element_type=F32)


def rms_round(values):
    scale = lax.rsqrt(jnp.mean(values * values, axis=-1, keepdims=True) + EPS)
    return (values * scale).astype(BF)


def body(
    len_ref, occ_ref, x_hbm, bm_hbm, sm_hbm, wg_hbm, wd_hbm, o_ref,
    x_ref, bm_ref, sm_ref, wg_ref, wd_ref,
    lens_rx, gu_tx, gu_rx, wd_tx, wd_rx, zunit_gu, zunit_wd, gu_lo, gu_hi, wd_lo, wd_hi, xm, spread, pre, psel, picks,
    sums, scales, hid,
    fsend, frecv, p1tx, p1rx, p2tx, p2rx,
    lens_s, lens_r, gu_s, gu_r, wd_s, wd_r, z_s, z_r, tok_s, tok_r,
    p1_s, p1_r, p2_s, p2_r, ring_s, ring_r, core_s, core_r, own_s, in_s, keep_s, z2_s, z2_r,
):
    page, tok = lax.axis_index("page"), lax.axis_index("tok")
    x, z = div(page, NZ), mod(page, NZ)
    y, c = div(tok, NC), mod(tok, NC)
    yh, yl = div(y, 2), mod(y, 2)
    sibling = tok + 1 - 2 * c

    def rcopy(src, dst, ssem, rsem, to_page, to_tok):
        return pltpu.make_async_remote_copy(
            src_ref=src, dst_ref=dst, send_sem=ssem, recv_sem=rsem,
            device_id=(to_page, to_tok), device_id_type=MESH,
        )

    def wait_recv(ref, sem):
        rcopy(ref, ref, sem, sem, page, sibling).wait_recv()

    def wait_send(ref, sem):
        rcopy(ref, ref, sem, sem, page, sibling).wait_send()

    loads = [
        pltpu.make_async_copy(src, dst, in_s.at[i])
        for i, (src, dst) in enumerate(
            [(wg_hbm, wg_ref), (wd_hbm, wd_ref), (x_hbm, x_ref), (bm_hbm, bm_ref), (sm_hbm, sm_ref)]
        )
    ]
    for load in loads:
        load.start()
    barrier = pltpu.get_barrier_semaphore()

    @pl.loop(1, PAGES)
    def _(k):
        pl.semaphore_signal(barrier, inc=1, device_id=(mod(page + k, PAGES), tok), device_id_type=MESH)

    @pl.loop(1, TOKS)
    def _(k):
        pl.semaphore_signal(barrier, inc=1, device_id=(page, mod(tok + k, TOKS)), device_id_type=MESH)

    length = len_ref[0]
    loads[0].wait()
    loads[1].wait()
    place8 = (iota((16, 8), 0) == iota((16, 8), 1) + 8 * c).astype(BF)
    place4 = (iota((16, 4), 0) == iota((16, 4), 1) + 4 * mod(tok, 4)).astype(BF)
    for g in range(2):
        gu_tx[g] = matmul(place8, wg_ref[g]).astype(BF)
    wd_all = matmul(place4, wd_ref[...]).astype(BF)
    for q in range(4):
        wd_tx[q] = wd_all[:, q * 512 : (q + 1) * 512]
    lens_rx[page] = jnp.full((1, 128), length, jnp.int32)

    loads[2].wait()
    loads[3].wait()
    for b in range(4):
        limit = length * occ_ref[0, b] - tok * ROWS - b * BLK
        rows = slice(b * BLK, (b + 1) * BLK)
        live = iota((BLK, D), 0) < limit
        masked = jnp.where(live, x_ref[rows, :].astype(F32), 0.0)
        xm[rows, :] = masked.astype(BF)
        first = matmul(bm_ref[b], rms_round(masked)).astype(BF)
        for h, (at, n) in enumerate(CHUNKS):
            fsend[h][:, b] = first[:, at : at + n].reshape(TOKS, PER, n)

    pl.semaphore_wait(barrier, PAGES - 1 + TOKS - 1)

    rcopy(gu_tx.at[1 - c], gu_rx, gu_s, gu_r, page, sibling).start()
    half = 4 * div(tok, 4)
    for k in range(1, 4):
        q = mod(tok + k, 4)
        rcopy(wd_tx.at[q], wd_rx.at[3 - k], wd_s, wd_r, page, half + q).start()

    own = []

    def send_first(h):
        own.append(pltpu.make_async_copy(fsend[h].at[tok], frecv[h].at[tok], own_s.at[h]))
        own[h].start()

        @pl.loop(1, TOKS)
        def _(k):
            to = mod(tok + k, TOKS)
            rcopy(fsend[h].at[to], frecv[h].at[tok], tok_s.at[h], tok_r.at[h], page, to).start()

    send_first(0)

    @pl.loop(1, PAGES)
    def _(k):
        rcopy(lens_rx.at[page], lens_rx.at[page], lens_s, lens_r, mod(page + k, PAGES), tok).start()

    wait_recv(gu_rx, gu_r)
    wait_recv(wd_rx, wd_r)
    zunit_gu[z] = gu_tx[c] + gu_rx[...]
    zunit_wd[z] = wd_tx[mod(tok, 4)] + wd_rx[0] + wd_rx[1] + wd_rx[2]
    zunits = [zunit_gu, zunit_wd]

    def z_copy(kind, origin, by, ssem, rsem):
        ref = zunits[kind].at[mod(z + origin + NZ, NZ)]
        return rcopy(ref, ref, ssem.at[kind], rsem.at[kind], x * NZ + mod(z + by + NZ, NZ), tok)

    for kind in range(2):
        for by in (2, -2, 1, -1):
            z_copy(kind, 0, by, z_s, z_r).start()
    send_first(1)
    send_first(2)

    loads[4].wait()
    expand = (iota((NB, ROWS), 0) == iota((NB, ROWS), 1) >> 4).astype(BF)
    wide = matmul(sm_ref[...].reshape(ROWS, NB), expand)
    same = (iota((ROWS, ROWS), 1) & 15) == (iota((ROWS, ROWS), 0) >> 5)
    spread[...] = jnp.where(same, wide, 0.0).astype(BF)

    wait_recv(lens_rx.at[pl.ds(0, PAGES - 1)], lens_r)
    lens = lens_rx[:, 0, :]
    lens = jnp.concatenate([lens] * 4, axis=1)
    kept = jnp.clip(lens - tok * ROWS, 0, ROWS)
    who = iota((PAGES, ROWS), 0)
    lane_page = iota((PAGES, ROWS), 1) >> 4
    shift = jnp.sum(jnp.where(who < page, kept, 0), axis=0, keepdims=True)
    start_of = jnp.sum(jnp.where(who < lane_page, kept, 0), axis=0, keepdims=True)
    stop_of = start_of + jnp.sum(jnp.where(who == lane_page, kept, 0), axis=0, keepdims=True)

    @pl.loop(0, 4)
    def _(r):
        rows = pl.ds(pl.multiple_of(r * 128, 128), 128)
        slot = iota((128, ROWS), 0) + r * 128
        turn = (((iota((128, ROWS), 1) + shift) & (ROWS - 1)) == slot).astype(BF)
        pre[rows, :] = matmul(turn, xm[...]).astype(BF)
        psel[rows, :] = matmul(turn, spread[...]).astype(BF)

    los, his = [gu_lo, wd_lo], [gu_hi, wd_hi]

    def xlo(xx, cut, kind):
        n = SPLITS[kind]
        zs = [pl.ds(0, n), pl.ds(0, n // 2), pl.ds(n // 2, n - n // 2)][cut]
        return los[kind].at[c, yh, yl, xx, zs]

    def yhi(yy, cut, kind):
        n = NZ - SPLITS[kind]
        mid = (n + 1) // 2
        zs = [pl.ds(0, n), pl.ds(0, mid), pl.ds(mid, n - mid)][cut]
        return his[kind].at[c, x, div(yy, 2), mod(yy, 2), zs]

    def ylo(yy, cut, kind):
        xs = [pl.ds(0, 4), pl.ds(0, 2), pl.ds(2, 2)][cut]
        return los[kind].at[c, div(yy, 2), mod(yy, 2), xs]

    def xhi(xx, cut, kind):
        ys = [pl.ds(0, 2), pl.ds(0, 1), pl.ds(1, 1)][cut]
        return his[kind].at[c, xx, ys]

    def xdev(by):
        return mod(x + by, NX) * NZ + z, tok

    def ydev(by):
        return page, mod(y + by, NY) * NC + c

    rings = [[(xlo, x, xdev), (yhi, y, ydev)], [(ylo, y, ydev), (xhi, x, xdev)]]

    def ring_copy(stage, kind, hop, which, way):
        piece, me, dev = rings[stage][which]
        by = 1 if way == 0 else 3
        ref = piece(me, 0, kind) if hop == 0 else piece(mod(me + 4 - by, 4), 1 + way, kind)
        src = ref
        if stage == 0 and hop == 0:
            src = zunits[kind].at[pl.ds(0, SPLITS[kind]) if which == 0 else pl.ds(SPLITS[kind], NZ - SPLITS[kind])]
        i = stage * 16 + kind * 8 + hop * 4 + which * 2 + way
        return rcopy(src, ref, ring_s.at[i], ring_r.at[i], *dev(by))

    def arriving(stage, kind, hop, which, way):
        piece, me, dev = rings[stage][which]
        by = 1 if way == 0 else 3
        return piece(mod(me + 4 - by, 4), 0, kind) if hop == 0 else piece(mod(me + 2, 4), 1 + way, kind)

    def ring_arrived(stage, kind, hop, which, way):
        i = stage * 16 + kind * 8 + hop * 4 + which * 2 + way
        wait_recv(arriving(stage, kind, hop, which, way), ring_r.at[i])

    def pass_on(kind, which, by, src=None):
        j = mod((x, y)[which] + by, 4)
        ref = (los[kind].at[c, yh, yl, j], his[kind].at[c, x, div(j, 2), mod(j, 2)])[which]
        for way in range(2):
            i = 16 + kind * 8 + which * 2 + way
            dev = (ydev, xdev)[which](1 if way == 0 else 3)
            rcopy(ref if src is None else src, ref, ring_s.at[i], ring_r.at[i], *dev).start()

    both = [(which, way) for which in range(2) for way in range(2)]

    def core_copy(i, ref):
        copy = rcopy(ref, ref, core_s.at[i], core_r.at[i], page, sibling)
        copy.start()
        return copy

    def turn_rows(h):
        at, n = CHUNKS[h]
        own[h].wait()
        wait_recv(frecv[h].at[pl.ds(0, TOKS - 1)], tok_r.at[h])

        @pl.loop(0, 4)
        def _(r):
            rows = pl.ds(pl.multiple_of(r * 128, 128), 128)
            second = matmul(psel[rows, :], frecv[h][...].reshape(ROWS, n))
            mixed = (pre[rows, at : at + n].astype(F32) + second).astype(BF)
            p1tx[h][pl.ds(r * 8, 8)] = mixed.reshape(8, PER, n)

        @pl.loop(1, PAGES)
        def _(k):
            to = mod(page + k, PAGES)
            rcopy(p1tx[h].at[to], p1rx[h].at[page], p1_s.at[h], p1_r.at[h], to, tok).start()

        own1.append(pltpu.make_async_copy(p1tx[h].at[page], p1rx[h].at[page], own_s.at[3 + h]))
        own1[h].start()

    def pack_rows(h):
        n = CHUNKS[h][1]
        own1[h].wait()
        wait_recv(p1rx[h].at[pl.ds(0, PAGES - 1)], p1_r.at[h])

        @pl.loop(0, 4)
        def _(r):
            rows = pl.ds(pl.multiple_of(r * 128, 128), 128)
            mixed = matmul(picks[rows, :], p1rx[h][...].reshape(ROWS, n))
            p2tx[h][pl.ds(r * 8, 8)] = mixed.astype(BF).reshape(8, PER, n)

        @pl.loop(1, PAGES)
        def _(k):
            to = mod(page + k, PAGES)
            rcopy(p2tx[h].at[to], p2rx[h].at[page], p2_s.at[h], p2_r.at[h], to, tok).start()

        own2.append(pltpu.make_async_copy(p2tx[h].at[page], p2rx[h].at[page], own_s.at[6 + h]))
        own2[h].start()

    own1, own2, keeps, cores = [], [], [], [[], []]
    for kind in range(2):
        wait_recv(zunits[kind].at[pl.ds(0, 4)], z_r.at[kind])
        z_copy(kind, -2, 1, z2_s, z2_r).start()
        z_copy(kind, 2, -1, z2_s, z2_r).start()
        z_copy(kind, 4 * kind - 2, 2 - 4 * kind, z2_s, z2_r).start()
    turn_rows(0)
    for kind in range(2):
        wait_recv(zunits[kind].at[pl.ds(0, 3)], z2_r.at[kind])
        for which, way in both:
            ring_copy(0, kind, 0, which, way).start()
        for which in range(2):
            piece, me, dev = rings[0][which]
            span = pl.ds(0, SPLITS[kind]) if which == 0 else pl.ds(SPLITS[kind], NZ - SPLITS[kind])
            copy = pltpu.make_async_copy(zunits[kind].at[span], piece(me, 0, kind), keep_s.at[kind * 2 + which])
            copy.start()
            pass_on(kind, which, 0, zunits[kind].at[span])
            keeps.append(copy)
    turn_rows(1)
    for kind in range(2):
        for which, way in both:
            ring_arrived(0, kind, 0, which, way)
            ring_copy(0, kind, 1, which, way).start()
        for which, way in both:
            pass_on(kind, which, 3 if way == 0 else 1)
    for copy in keeps:
        copy.wait()
    turn_rows(2)

    @pl.loop(0, 4)
    def _(r):
        row = iota((128, ROWS), 0) + r * 128
        col = iota((128, ROWS), 1)
        target = (row >> 4) * ROWS + page * PER + (row & 15)
        pick = ((row & 15) == (col & 15)) & (target >= start_of) & (target < stop_of)
        picks[pl.ds(pl.multiple_of(r * 128, 128), 128), :] = pick.astype(BF)

    for kind in range(2):
        for which, way in both:
            ring_arrived(0, kind, 1, which, way)
        for which in range(2):
            pass_on(kind, which, 2)
    pack_rows(0)
    for kind in range(2):
        for which in range(2):
            piece, me, dev = rings[1][which]
            cores[kind].append(core_copy(kind * 10 + which, piece(me, 0, kind)))
    pack_rows(1)
    for kind in range(2):
        for which, way in both:
            ring_arrived(1, kind, 0, which, way)
            ring_copy(1, kind, 1, which, way).start()
            cores[kind].append(core_copy(kind * 10 + 2 + which * 2 + way, arriving(1, kind, 0, which, way)))
        if kind == 0:
            pack_rows(2)

    def last_hop(kind):
        for which, way in both:
            ring_arrived(1, kind, 1, which, way)
            cores[kind].append(core_copy(kind * 10 + 6 + which * 2 + way, arriving(1, kind, 1, which, way)))

    last_hop(0)

    def packed_chunk(h):
        return p2rx[h][...].reshape(ROWS, CHUNKS[h][1])

    def squares(h):
        wide = packed_chunk(h).astype(F32)
        return jnp.sum(wide * wide, axis=-1, keepdims=True)

    def unit(kind, core, xx, zz, ys, cols):
        if zz < SPLITS[kind]:
            return los[kind][core, :, ys, xx, zz, :, cols]
        return his[kind][core, xx, :, ys, zz - SPLITS[kind], :, cols]

    def gate_rows(core, xx, t, cols, n):
        parts = [unit(0, core, xx, zz, slice(None), cols).reshape(64, n) for zz in range(4 * t, 4 * t + 4)]
        return jnp.concatenate(parts, axis=0)

    def arrived_chunk(h):
        own2[h].wait()
        wait_recv(p2rx[h].at[pl.ds(0, PAGES - 1)], p2_r.at[h])

    for copy in cores[0]:
        copy.wait_recv()
    arrived_chunk(0)
    arrived_chunk(1)

    @pl.loop(0, 4)
    def _(xx):
        for t in range(2):
            cols = pl.ds(pl.multiple_of(xx * 512 + t * 256, 256), 256)
            for core in range(2):
                sums[core, :, cols] = sum(
                    matmul_nt(packed_chunk(h), gate_rows(core, xx, t, slice(h * 256, h * 256 + 256), 256)) for h in range(2)
                )

    first_squares = squares(0) + squares(1)
    last_hop(1)
    arrived_chunk(2)
    scale = lax.rsqrt((first_squares + squares(2)) / D + EPS)
    scales[...] = jnp.broadcast_to(scale, (ROWS, 256))

    @pl.loop(0, 4)
    def _(xx):
        for t in range(2):
            cols = pl.ds(pl.multiple_of(xx * 512 + t * 256, 256), 256)
            gate, up = [
                (sums[core, :, cols] + matmul_nt(packed_chunk(2), gate_rows(core, xx, t, slice(512, D), 512))) * scales[...]
                for core in range(2)
            ]
            hid[:, cols] = (gate / (1.0 + jnp.exp(-gate)) * up).astype(BF)

    for copy in cores[1]:
        copy.wait_recv()

    for t, h in enumerate((0, 1, 2, 2)):
        at = t * 256 - CHUNKS[h][0]
        total = p2rx[h][:, :, at : at + 256].reshape(ROWS, 256).astype(F32)
        for q in range(4):
            down = jnp.concatenate([unit(1, q % 2, t, zz, q // 2, slice(None)).reshape(32, 512) for zz in range(NZ)], axis=0)
            total = total + matmul_nt(hid[:, q * 512 : (q + 1) * 512], down)
        o_ref[:, t * 256 : (t + 1) * 256] = total.astype(BF)

    wait_send(gu_rx, gu_s)
    wait_send(wd_rx, wd_s)
    wait_send(lens_rx.at[pl.ds(0, PAGES - 1)], lens_s)
    for kind in range(2):
        wait_send(zunits[kind].at[pl.ds(0, 4)], z_s.at[kind])
        wait_send(zunits[kind].at[pl.ds(0, 3)], z2_s.at[kind])
    for h in range(len(CHUNKS)):
        wait_send(frecv[h].at[pl.ds(0, TOKS - 1)], tok_s.at[h])
        wait_send(p1tx[h].at[pl.ds(0, PAGES - 1)], p1_s.at[h])
        wait_send(p2tx[h].at[pl.ds(0, PAGES - 1)], p2_s.at[h])
    for stage in range(2):
        for kind in range(2):
            for hop in range(2):
                for which, way in both:
                    ring_copy(stage, kind, hop, which, way).wait_send()
    for copy in cores[0] + cores[1]:
        copy.wait_send()


def per_device(tile_tokens, page_lengths, occupancy, block_mix, stride_mix, w_gate_up, w_down):
    vmem = pl.BlockSpec(memory_space=pltpu.VMEM)
    smem = pl.BlockSpec(memory_space=pltpu.SMEM)
    dma = pltpu.SemaphoreType.DMA
    anywhere = pl.BlockSpec(memory_space=pltpu.HBM)
    packed = pl.pallas_call(
        body,
        out_shape=jax.ShapeDtypeStruct((ROWS, D), BF),
        in_specs=[smem, smem] + [anywhere] * 5,
        out_specs=vmem,
        scratch_shapes=[
            pltpu.VMEM((ROWS, D), BF),
            pltpu.VMEM((4, BLK, BLK), BF),
            pltpu.VMEM((PER, NB, NB), BF),
            pltpu.VMEM((2, 8, D), BF),
            pltpu.VMEM((4, FF), BF),
            pltpu.VMEM((PAGES, 1, 128), jnp.int32),
            pltpu.VMEM((2, 16, D), BF),
            pltpu.VMEM((16, D), BF),
            pltpu.VMEM((4, 16, 512), BF),
            pltpu.VMEM((3, 16, 512), BF),
            pltpu.VMEM((NZ, 16, D), BF),
            pltpu.VMEM((NZ, 16, 512), BF),
            pltpu.VMEM((NC, 2, 2, NX, SPLITS[0], 16, D), BF),
            pltpu.VMEM((NC, NX, 2, 2, NZ - SPLITS[0], 16, D), BF),
            pltpu.VMEM((NC, 2, 2, NX, SPLITS[1], 16, 512), BF),
            pltpu.VMEM((NC, NX, 2, 2, NZ - SPLITS[1], 16, 512), BF),
            pltpu.VMEM((ROWS, D), BF),
            pltpu.VMEM((ROWS, ROWS), BF),
            pltpu.VMEM((ROWS, D), BF),
            pltpu.VMEM((ROWS, ROWS), BF),
            pltpu.VMEM((ROWS, ROWS), BF),
            pltpu.VMEM((2, ROWS, FF), F32),
            pltpu.VMEM((ROWS, 256), F32),
            pltpu.VMEM((ROWS, FF), BF),
            *[[pltpu.VMEM((TOKS, 4, PER, n), BF) for at, n in CHUNKS] for k in range(2)],
            *[[pltpu.VMEM((PAGES, PER, n), BF) for at, n in CHUNKS] for k in range(4)],
        ]
        + [dma] * 6
        + [dma((2,))] * 2
        + [dma((3,))] * 6
        + [dma((32,)), dma((32,)), dma((20,)), dma((20,)), dma((9,)), dma((5,)), dma((4,)), dma((2,)), dma((2,))],
        compiler_params=pltpu.CompilerParams(
            collective_id=0, has_side_effects=True, vmem_limit_bytes=48 * 1024 * 1024
        ),
    )(
        page_lengths, occupancy,
        *(
            pltpu.with_memory_space_constraint(v, pltpu.HBM)
            for v in (tile_tokens[0], block_mix, stride_mix, jnp.swapaxes(w_gate_up, 1, 2), w_down.T)
        ),
    )
    return packed.reshape(1, ROWS, D)


def solution(mesh):
    return jax.shard_map(
        per_device,
        mesh=mesh,
        in_specs=(
            P("page", "tok", None),
            P("page"),
            P("page", "tok"),
            P("tok", None, None),
            P("tok", None, None),
            P(None, None, ("page", "tok")),
            P(None, ("page", "tok")),
        ),
        out_specs=P("tok", "page", None),
        check_vma=False,
    )
```

```python
import jax
import jax.numpy as jnp
from jax import lax
from jax.experimental import pallas as pl
from jax.experimental.pallas import tpu as pltpu
from jax.sharding import PartitionSpec as P

NX, NZ, NY, NC = 4, 8, 4, 2
PAGES, TOKS = 32, 8
ROWS, D, FF = 512, 1024, 2048
BLK, NB, PER = 128, 32, 16
EPS = 1e-05
SPLITS = (6, 5)
CHUNKS = ((0, 256), (256, 256), (512, 512))
MESH = pl.DeviceIdType.MESH
NT = (((1,), (1,)), ((), ()))
BF, F32 = jnp.bfloat16, jnp.float32


def mod(a, n):
    return lax.rem(a, jnp.int32(n))


def div(a, n):
    return lax.div(a, jnp.int32(n))


def iota(shape, dim):
    return lax.broadcasted_iota(jnp.int32, shape, dim)


def matmul(a, b):
    return jnp.dot(a, b, preferred_element_type=F32)


def matmul_nt(a, b):
    return lax.dot_general(a, b, NT, preferred_element_type=F32)


def rms_round(values):
    scale = lax.rsqrt(jnp.mean(values * values, axis=-1, keepdims=True) + EPS)
    return (values * scale).astype(BF)


def body(
    len_ref, occ_hbm, x_hbm, bm_hbm, sm_hbm, wg_hbm, wd_hbm, o_ref,
    occ_ref, x_ref, bm_ref, sm_ref, wg_ref, wd_ref,
    lens_rx, gu_tx, gu_rx, wd_tx, wd_rx, zunit_gu, zunit_wd, gu_lo, gu_hi, wd_lo, wd_hi, xm, spread, pre, psel, picks,
    sums, scales, hid,
    fsend, frecv, p1tx, p1rx, p2tx, p2rx,
    lens_s, lens_r, gu_s, gu_r, wd_s, wd_r, z_s, z_r, tok_s, tok_r,
    p1_s, p1_r, p2_s, p2_r, ring_s, ring_r, core_s, core_r, own_s, in_s, keep_s, z2_s, z2_r,
):
    page, tok = lax.axis_index("page"), lax.axis_index("tok")
    x, z = div(page, NZ), mod(page, NZ)
    y, c = div(tok, NC), mod(tok, NC)
    yh, yl = div(y, 2), mod(y, 2)
    sibling = tok + 1 - 2 * c

    def rcopy(src, dst, ssem, rsem, to_page, to_tok):
        return pltpu.make_async_remote_copy(
            src_ref=src, dst_ref=dst, send_sem=ssem, recv_sem=rsem,
            device_id=(to_page, to_tok), device_id_type=MESH,
        )

    def wait_recv(ref, sem):
        rcopy(ref, ref, sem, sem, page, sibling).wait_recv()

    def wait_send(ref, sem):
        rcopy(ref, ref, sem, sem, page, sibling).wait_send()

    loads = [
        pltpu.make_async_copy(src, dst, in_s.at[i])
        for i, (src, dst) in enumerate(
            [
                (wg_hbm, wg_ref), (wd_hbm, wd_ref), (x_hbm, x_ref), (bm_hbm, bm_ref), (sm_hbm, sm_ref),
                (occ_hbm, occ_ref),
            ]
        )
    ]
    for load in loads:
        load.start()
    barrier = pltpu.get_barrier_semaphore()

    @pl.loop(1, PAGES)
    def _(k):
        pl.semaphore_signal(barrier, inc=1, device_id=(mod(page + k, PAGES), tok), device_id_type=MESH)

    @pl.loop(1, TOKS)
    def _(k):
        pl.semaphore_signal(barrier, inc=1, device_id=(page, mod(tok + k, TOKS)), device_id_type=MESH)

    length = len_ref[0]
    loads[0].wait()
    loads[1].wait()
    place8 = (iota((16, 8), 0) == iota((16, 8), 1) + 8 * c).astype(BF)
    place4 = (iota((16, 4), 0) == iota((16, 4), 1) + 4 * mod(tok, 4)).astype(BF)
    for g in range(2):
        gu_tx[g] = matmul(place8, wg_ref[g]).astype(BF)
    wd_all = matmul(place4, wd_ref[...]).astype(BF)
    for q in range(4):
        wd_tx[q] = wd_all[:, q * 512 : (q + 1) * 512]
    lens_rx[page] = jnp.full((1, 128), length, jnp.int32)

    loads[2].wait()
    loads[3].wait()
    loads[5].wait()
    for b in range(4):
        limit = length * occ_ref[:, b : b + 1] - tok * ROWS - b * BLK
        rows = slice(b * BLK, (b + 1) * BLK)
        live = iota((BLK, D), 0) < limit
        masked = jnp.where(live, x_ref[rows, :].astype(F32), 0.0)
        xm[rows, :] = masked.astype(BF)
        first = matmul(bm_ref[b], rms_round(masked)).astype(BF)
        for h, (at, n) in enumerate(CHUNKS):
            fsend[h][:, b] = first[:, at : at + n].reshape(TOKS, PER, n)

    pl.semaphore_wait(barrier, PAGES - 1 + TOKS - 1)

    rcopy(gu_tx.at[1 - c], gu_rx, gu_s, gu_r, page, sibling).start()
    half = 4 * div(tok, 4)
    for k in range(1, 4):
        q = mod(tok + k, 4)
        rcopy(wd_tx.at[q], wd_rx.at[3 - k], wd_s, wd_r, page, half + q).start()

    own = []

    def send_first(h):
        own.append(pltpu.make_async_copy(fsend[h].at[tok], frecv[h].at[tok], own_s.at[h]))
        own[h].start()

        @pl.loop(1, TOKS)
        def _(k):
            to = mod(tok + k, TOKS)
            rcopy(fsend[h].at[to], frecv[h].at[tok], tok_s.at[h], tok_r.at[h], page, to).start()

    send_first(0)

    @pl.loop(1, PAGES)
    def _(k):
        rcopy(lens_rx.at[page], lens_rx.at[page], lens_s, lens_r, mod(page + k, PAGES), tok).start()

    wait_recv(gu_rx, gu_r)
    wait_recv(wd_rx, wd_r)
    zunit_gu[z] = gu_tx[c] + gu_rx[...]
    zunit_wd[z] = wd_tx[mod(tok, 4)] + wd_rx[0] + wd_rx[1] + wd_rx[2]
    zunits = [zunit_gu, zunit_wd]

    def z_copy(kind, origin, by, ssem, rsem):
        ref = zunits[kind].at[mod(z + origin + NZ, NZ)]
        return rcopy(ref, ref, ssem.at[kind], rsem.at[kind], x * NZ + mod(z + by + NZ, NZ), tok)

    for kind in range(2):
        for by in (2, -2, 1, -1):
            z_copy(kind, 0, by, z_s, z_r).start()
    send_first(1)
    send_first(2)

    loads[4].wait()
    expand = (iota((NB, ROWS), 0) == iota((NB, ROWS), 1) >> 4).astype(BF)
    wide = matmul(sm_ref[...].reshape(ROWS, NB), expand)
    same = (iota((ROWS, ROWS), 1) & 15) == (iota((ROWS, ROWS), 0) >> 5)
    spread[...] = jnp.where(same, wide, 0.0).astype(BF)

    wait_recv(lens_rx.at[pl.ds(0, PAGES - 1)], lens_r)
    lens = lens_rx[:, 0, :]
    lens = jnp.concatenate([lens] * 4, axis=1)
    kept = jnp.clip(lens - tok * ROWS, 0, ROWS)
    who = iota((PAGES, ROWS), 0)
    lane_page = iota((PAGES, ROWS), 1) >> 4
    shift = jnp.sum(jnp.where(who < page, kept, 0), axis=0, keepdims=True)
    start_of = jnp.sum(jnp.where(who < lane_page, kept, 0), axis=0, keepdims=True)
    stop_of = start_of + jnp.sum(jnp.where(who == lane_page, kept, 0), axis=0, keepdims=True)

    @pl.loop(0, 4)
    def _(r):
        rows = pl.ds(pl.multiple_of(r * 128, 128), 128)
        slot = iota((128, ROWS), 0) + r * 128
        turn = (((iota((128, ROWS), 1) + shift) & (ROWS - 1)) == slot).astype(BF)
        pre[rows, :] = matmul(turn, xm[...]).astype(BF)
        psel[rows, :] = matmul(turn, spread[...]).astype(BF)

    los, his = [gu_lo, wd_lo], [gu_hi, wd_hi]

    def xlo(xx, cut, kind):
        n = SPLITS[kind]
        zs = [pl.ds(0, n), pl.ds(0, n // 2), pl.ds(n // 2, n - n // 2)][cut]
        return los[kind].at[c, yh, yl, xx, zs]

    def yhi(yy, cut, kind):
        n = NZ - SPLITS[kind]
        mid = (n + 1) // 2
        zs = [pl.ds(0, n), pl.ds(0, mid), pl.ds(mid, n - mid)][cut]
        return his[kind].at[c, x, div(yy, 2), mod(yy, 2), zs]

    def ylo(yy, cut, kind):
        xs = [pl.ds(0, 4), pl.ds(0, 2), pl.ds(2, 2)][cut]
        return los[kind].at[c, div(yy, 2), mod(yy, 2), xs]

    def xhi(xx, cut, kind):
        ys = [pl.ds(0, 2), pl.ds(0, 1), pl.ds(1, 1)][cut]
        return his[kind].at[c, xx, ys]

    def xdev(by):
        return mod(x + by, NX) * NZ + z, tok

    def ydev(by):
        return page, mod(y + by, NY) * NC + c

    rings = [[(xlo, x, xdev), (yhi, y, ydev)], [(ylo, y, ydev), (xhi, x, xdev)]]

    def ring_copy(stage, kind, hop, which, way):
        piece, me, dev = rings[stage][which]
        by = 1 if way == 0 else 3
        ref = piece(me, 0, kind) if hop == 0 else piece(mod(me + 4 - by, 4), 1 + way, kind)
        src = ref
        if stage == 0 and hop == 0:
            src = zunits[kind].at[pl.ds(0, SPLITS[kind]) if which == 0 else pl.ds(SPLITS[kind], NZ - SPLITS[kind])]
        i = stage * 16 + kind * 8 + hop * 4 + which * 2 + way
        return rcopy(src, ref, ring_s.at[i], ring_r.at[i], *dev(by))

    def arriving(stage, kind, hop, which, way):
        piece, me, dev = rings[stage][which]
        by = 1 if way == 0 else 3
        return piece(mod(me + 4 - by, 4), 0, kind) if hop == 0 else piece(mod(me + 2, 4), 1 + way, kind)

    def ring_arrived(stage, kind, hop, which, way):
        i = stage * 16 + kind * 8 + hop * 4 + which * 2 + way
        wait_recv(arriving(stage, kind, hop, which, way), ring_r.at[i])

    def pass_on(kind, which, by, src=None):
        j = mod((x, y)[which] + by, 4)
        ref = (los[kind].at[c, yh, yl, j], his[kind].at[c, x, div(j, 2), mod(j, 2)])[which]
        for way in range(2):
            i = 16 + kind * 8 + which * 2 + way
            dev = (ydev, xdev)[which](1 if way == 0 else 3)
            rcopy(ref if src is None else src, ref, ring_s.at[i], ring_r.at[i], *dev).start()

    both = [(which, way) for which in range(2) for way in range(2)]

    def core_copy(i, ref):
        copy = rcopy(ref, ref, core_s.at[i], core_r.at[i], page, sibling)
        copy.start()
        return copy

    def turn_rows(h):
        at, n = CHUNKS[h]
        own[h].wait()
        wait_recv(frecv[h].at[pl.ds(0, TOKS - 1)], tok_r.at[h])

        @pl.loop(0, 4)
        def _(r):
            rows = pl.ds(pl.multiple_of(r * 128, 128), 128)
            second = matmul(psel[rows, :], frecv[h][...].reshape(ROWS, n))
            mixed = (pre[rows, at : at + n].astype(F32) + second).astype(BF)
            p1tx[h][pl.ds(r * 8, 8)] = mixed.reshape(8, PER, n)

        @pl.loop(1, PAGES)
        def _(k):
            to = mod(page + k, PAGES)
            rcopy(p1tx[h].at[to], p1rx[h].at[page], p1_s.at[h], p1_r.at[h], to, tok).start()

        own1.append(pltpu.make_async_copy(p1tx[h].at[page], p1rx[h].at[page], own_s.at[3 + h]))
        own1[h].start()

    def pack_rows(h):
        n = CHUNKS[h][1]
        own1[h].wait()
        wait_recv(p1rx[h].at[pl.ds(0, PAGES - 1)], p1_r.at[h])

        @pl.loop(0, 4)
        def _(r):
            rows = pl.ds(pl.multiple_of(r * 128, 128), 128)
            mixed = matmul(picks[rows, :], p1rx[h][...].reshape(ROWS, n))
            p2tx[h][pl.ds(r * 8, 8)] = mixed.astype(BF).reshape(8, PER, n)

        @pl.loop(1, PAGES)
        def _(k):
            to = mod(page + k, PAGES)
            rcopy(p2tx[h].at[to], p2rx[h].at[page], p2_s.at[h], p2_r.at[h], to, tok).start()

        own2.append(pltpu.make_async_copy(p2tx[h].at[page], p2rx[h].at[page], own_s.at[6 + h]))
        own2[h].start()

    own1, own2, keeps, cores = [], [], [], [[], []]
    for kind in range(2):
        wait_recv(zunits[kind].at[pl.ds(0, 4)], z_r.at[kind])
        z_copy(kind, -2, 1, z2_s, z2_r).start()
        z_copy(kind, 2, -1, z2_s, z2_r).start()
        z_copy(kind, 4 * kind - 2, 2 - 4 * kind, z2_s, z2_r).start()
    turn_rows(0)
    for kind in range(2):
        wait_recv(zunits[kind].at[pl.ds(0, 3)], z2_r.at[kind])
        for which, way in both:
            ring_copy(0, kind, 0, which, way).start()
        for which in range(2):
            piece, me, dev = rings[0][which]
            span = pl.ds(0, SPLITS[kind]) if which == 0 else pl.ds(SPLITS[kind], NZ - SPLITS[kind])
            copy = pltpu.make_async_copy(zunits[kind].at[span], piece(me, 0, kind), keep_s.at[kind * 2 + which])
            copy.start()
            pass_on(kind, which, 0, zunits[kind].at[span])
            keeps.append(copy)
    turn_rows(1)
    for kind in range(2):
        for which, way in both:
            ring_arrived(0, kind, 0, which, way)
            ring_copy(0, kind, 1, which, way).start()
        for which, way in both:
            pass_on(kind, which, 3 if way == 0 else 1)
    for copy in keeps:
        copy.wait()
    turn_rows(2)

    @pl.loop(0, 4)
    def _(r):
        row = iota((128, ROWS), 0) + r * 128
        col = iota((128, ROWS), 1)
        target = (row >> 4) * ROWS + page * PER + (row & 15)
        pick = ((row & 15) == (col & 15)) & (target >= start_of) & (target < stop_of)
        picks[pl.ds(pl.multiple_of(r * 128, 128), 128), :] = pick.astype(BF)

    for kind in range(2):
        for which, way in both:
            ring_arrived(0, kind, 1, which, way)
        for which in range(2):
            pass_on(kind, which, 2)
    pack_rows(0)
    for kind in range(2):
        for which in range(2):
            piece, me, dev = rings[1][which]
            cores[kind].append(core_copy(kind * 10 + which, piece(me, 0, kind)))
    pack_rows(1)
    for kind in range(2):
        for which, way in both:
            ring_arrived(1, kind, 0, which, way)
            ring_copy(1, kind, 1, which, way).start()
            cores[kind].append(core_copy(kind * 10 + 2 + which * 2 + way, arriving(1, kind, 0, which, way)))
        if kind == 0:
            pack_rows(2)

    def last_hop(kind):
        for which, way in both:
            ring_arrived(1, kind, 1, which, way)
            cores[kind].append(core_copy(kind * 10 + 6 + which * 2 + way, arriving(1, kind, 1, which, way)))

    last_hop(0)

    def packed_chunk(h):
        return p2rx[h][...].reshape(ROWS, CHUNKS[h][1])

    def squares(h):
        wide = packed_chunk(h).astype(F32)
        return jnp.sum(wide * wide, axis=-1, keepdims=True)

    def unit(kind, core, xx, zz, ys, cols):
        if zz < SPLITS[kind]:
            return los[kind][core, :, ys, xx, zz, :, cols]
        return his[kind][core, xx, :, ys, zz - SPLITS[kind], :, cols]

    def gate_rows(core, xx, t, cols, n):
        parts = [unit(0, core, xx, zz, slice(None), cols).reshape(64, n) for zz in range(4 * t, 4 * t + 4)]
        return jnp.concatenate(parts, axis=0)

    def arrived_chunk(h):
        own2[h].wait()
        wait_recv(p2rx[h].at[pl.ds(0, PAGES - 1)], p2_r.at[h])

    for copy in cores[0]:
        copy.wait_recv()
    arrived_chunk(0)
    arrived_chunk(1)

    @pl.loop(0, 4)
    def _(xx):
        for t in range(2):
            cols = pl.ds(pl.multiple_of(xx * 512 + t * 256, 256), 256)
            for core in range(2):
                sums[core, :, cols] = sum(
                    matmul_nt(packed_chunk(h), gate_rows(core, xx, t, slice(h * 256, h * 256 + 256), 256)) for h in range(2)
                )

    first_squares = squares(0) + squares(1)
    last_hop(1)
    arrived_chunk(2)
    scale = lax.rsqrt((first_squares + squares(2)) / D + EPS)
    scales[...] = jnp.broadcast_to(scale, (ROWS, 256))

    @pl.loop(0, 4)
    def _(xx):
        for t in range(2):
            cols = pl.ds(pl.multiple_of(xx * 512 + t * 256, 256), 256)
            gate, up = [
                (sums[core, :, cols] + matmul_nt(packed_chunk(2), gate_rows(core, xx, t, slice(512, D), 512))) * scales[...]
                for core in range(2)
            ]
            hid[:, cols] = (gate / (1.0 + jnp.exp(-gate)) * up).astype(BF)

    for copy in cores[1]:
        copy.wait_recv()

    for t, h in enumerate((0, 1, 2, 2)):
        at = t * 256 - CHUNKS[h][0]
        total = p2rx[h][:, :, at : at + 256].reshape(ROWS, 256).astype(F32)
        for q in range(4):
            down = jnp.concatenate([unit(1, q % 2, t, zz, q // 2, slice(None)).reshape(32, 512) for zz in range(NZ)], axis=0)
            total = total + matmul_nt(hid[:, q * 512 : (q + 1) * 512], down)
        o_ref[:, t * 256 : (t + 1) * 256] = total.astype(BF)

    wait_send(gu_rx, gu_s)
    wait_send(wd_rx, wd_s)
    wait_send(lens_rx.at[pl.ds(0, PAGES - 1)], lens_s)
    for kind in range(2):
        wait_send(zunits[kind].at[pl.ds(0, 4)], z_s.at[kind])
        wait_send(zunits[kind].at[pl.ds(0, 3)], z2_s.at[kind])
    for h in range(len(CHUNKS)):
        wait_send(frecv[h].at[pl.ds(0, TOKS - 1)], tok_s.at[h])
        wait_send(p1tx[h].at[pl.ds(0, PAGES - 1)], p1_s.at[h])
        wait_send(p2tx[h].at[pl.ds(0, PAGES - 1)], p2_s.at[h])
    for stage in range(2):
        for kind in range(2):
            for hop in range(2):
                for which, way in both:
                    ring_copy(stage, kind, hop, which, way).wait_send()
    for copy in cores[0] + cores[1]:
        copy.wait_send()


def per_device(tile_tokens, page_lengths, occupancy, block_mix, stride_mix, w_gate_up, w_down):
    vmem = pl.BlockSpec(memory_space=pltpu.VMEM)
    smem = pl.BlockSpec(memory_space=pltpu.SMEM)
    dma = pltpu.SemaphoreType.DMA
    anywhere = pl.BlockSpec(memory_space=pltpu.HBM)
    packed = pl.pallas_call(
        body,
        out_shape=jax.ShapeDtypeStruct((ROWS, D), BF),
        in_specs=[smem] + [anywhere] * 6,
        out_specs=vmem,
        scratch_shapes=[
            pltpu.VMEM((1, 4), jnp.int32),
            pltpu.VMEM((ROWS, D), BF),
            pltpu.VMEM((4, BLK, BLK), BF),
            pltpu.VMEM((PER, NB, NB), BF),
            pltpu.VMEM((2, 8, D), BF),
            pltpu.VMEM((4, FF), BF),
            pltpu.VMEM((PAGES, 1, 128), jnp.int32),
            pltpu.VMEM((2, 16, D), BF),
            pltpu.VMEM((16, D), BF),
            pltpu.VMEM((4, 16, 512), BF),
            pltpu.VMEM((3, 16, 512), BF),
            pltpu.VMEM((NZ, 16, D), BF),
            pltpu.VMEM((NZ, 16, 512), BF),
            pltpu.VMEM((NC, 2, 2, NX, SPLITS[0], 16, D), BF),
            pltpu.VMEM((NC, NX, 2, 2, NZ - SPLITS[0], 16, D), BF),
            pltpu.VMEM((NC, 2, 2, NX, SPLITS[1], 16, 512), BF),
            pltpu.VMEM((NC, NX, 2, 2, NZ - SPLITS[1], 16, 512), BF),
            pltpu.VMEM((ROWS, D), BF),
            pltpu.VMEM((ROWS, ROWS), BF),
            pltpu.VMEM((ROWS, D), BF),
            pltpu.VMEM((ROWS, ROWS), BF),
            pltpu.VMEM((ROWS, ROWS), BF),
            pltpu.VMEM((2, ROWS, FF), F32),
            pltpu.VMEM((ROWS, 256), F32),
            pltpu.VMEM((ROWS, FF), BF),
            *[[pltpu.VMEM((TOKS, 4, PER, n), BF) for at, n in CHUNKS] for k in range(2)],
            *[[pltpu.VMEM((PAGES, PER, n), BF) for at, n in CHUNKS] for k in range(4)],
        ]
        + [dma] * 6
        + [dma((2,))] * 2
        + [dma((3,))] * 6
        + [dma((32,)), dma((32,)), dma((20,)), dma((20,)), dma((9,)), dma((6,)), dma((4,)), dma((2,)), dma((2,))],
        compiler_params=pltpu.CompilerParams(
            collective_id=0, has_side_effects=True, vmem_limit_bytes=48 * 1024 * 1024
        ),
    )(
        page_lengths,
        *(
            pltpu.with_memory_space_constraint(v, pltpu.HBM)
            for v in (occupancy, tile_tokens[0], block_mix, stride_mix, jnp.swapaxes(w_gate_up, 1, 2), w_down.T)
        ),
    )
    return packed.reshape(1, ROWS, D)


def solution(mesh):
    return jax.shard_map(
        per_device,
        mesh=mesh,
        in_specs=(
            P("page", "tok", None),
            P("page"),
            P("page", "tok"),
            P("tok", None, None),
            P("tok", None, None),
            P(None, None, ("page", "tok")),
            P(None, ("page", "tok")),
        ),
        out_specs=P("tok", "page", None),
        check_vma=False,
    )
```
